32 devices in a mesh: groups: 2 (over y), expert: 4 (over z), replica: 4 (over x, core).
Axes of the slice: x: 2, y: 2, z: 4, core: 2. Of those that a mesh axis runs over, the one named last changes fastest.
Arguments:
- tokens: bfloat16 [4096, 1024], P(('groups', 'expert', 'replica')), parts along dimension 0, may hold values from -6 to 6
- expert_ids: int32 [4096, 6], P(('groups', 'expert', 'replica')), parts along dimension 0, may hold values from 0 to 15, all different within a row; in each aligned block of 128 rows (0 to 127, 128 to 255, ...) at most 64 rows name the same one
- gate_probs: bfloat16 [4096, 6], P(('groups', 'expert', 'replica')), parts along dimension 0, may hold values from 0.099609375 to 0.59765625
- cotangent: bfloat16 [4096, 1024], P(('groups', 'expert', 'replica')), parts along dimension 0, may hold values from -1.5 to 1.5
- gate_up: bfloat16 [1024, 16, 1536], P(None, 'expert'), may hold values from -0.1875 to 0.1875
- down_weights: bfloat16 [768, 16, 1024], P(None, 'expert'), may hold values from -0.21875 to 0.21875
Outputs:
- combined: bfloat16 [4096, 1024], P(('groups', 'expert', 'replica')), parts along dimension 0
- token_gradient: bfloat16 [4096, 1024], P(('groups', 'expert', 'replica')), parts along dimension 0
- prob_gradient: float32 [4096, 6], P(('groups', 'expert', 'replica')), parts along dimension 0
- gate_up_gradient: float32 [2048, 16, 1536], P(('groups', 'replica'), 'expert'), parts along dimension 0
- down_gradient: float32 [1536, 16, 1024], P(('groups', 'replica'), 'expert'), parts along dimension 0
The draws below stay inside these ranges and needn't reach their ends.
There are 2 independent parts, one for each index of `groups`. The reference program is written for one: setup_inputs(seed, part) draws one part's arguments, and reference() takes and returns one part's arrays. A program takes and returns all parts, laid end to end along the dimension named above; an argument that names none is the same for every part. Nothing has to cross between parts.
Inputs may be any that keep to these rules, and one draw needn't show every extreme that they name: `expert_ids`: each row names 6 different experts. Within the rows of one device (aligned blocks of 128 rows) no expert is named by more than 64 rows, and in some block one expert is named by exactly 64 rows.
All inputs are finite; a program needn't handle non-finite values.
Results may differ from the reference program's by a relative error of at most 0.0064.
Values may be sent and summed in bfloat16 or wider, within the bound.
A program may use at most 128 MiB of HBM per device.

```python
import math
import jax
import jax.numpy as jnp
import numpy as np
from jax import lax

D = 1024
FF = 768
TOP = 6
EXPERTS = 16
TOK_DEV = 128
CAP = 64
TOKENS = 2048
N_EXPERT = 4
N_REPLICA = 4


def level_of(key, shape, split, low, top_value):
    loudness = 1.0
    for dim, shards_of in split:
        draws = jax.random.uniform(jax.random.fold_in(jax.random.fold_in(key, 6), dim), (shards_of,), jnp.float32, low / len(split), top_value / len(split))
        loudness = loudness * jnp.repeat(jnp.exp(draws), shape[dim] // shards_of).reshape((-1,) + (1,) * (len(shape) - 1 - dim))
    return loudness


def assign_block(stream_key, own, number, rows, count, top, reach, slope):
    order = jax.random.permutation(stream_key, count)
    heavy_load, common = portions_of(count, rows * top, reach, slope, True), portions_of(count, rows * top, reach, slope, False)
    places = jnp.arange(count)

    def named(tallies, offset_by):
        used = int((tallies > 0).sum())
        fixed = max(1, used // 4)
        passed = fixed + (places - fixed + offset_by * (used - fixed)) % max(1, count - fixed)
        return jnp.zeros((count,), jnp.int32).at[order[jnp.where(places < fixed, places, passed)]].set(jnp.asarray(tallies, jnp.int32))

    tallies = jnp.where(number % 4 == 0, named(heavy_load, number // 4), named(common, number - number // 4 - 1))
    mixed = jax.random.permutation(jax.random.fold_in(own, 3), count)
    source_of, sink = mixed[0:count // 2 * 2:2], mixed[1:count // 2 * 2:2]
    margin = jnp.minimum(tallies[source_of] - 1, reach - tallies[sink]) // 2
    margin = jnp.where((source_of == order[0]) | (sink == order[0]) | (tallies[sink] == 0), 0, jnp.maximum(margin, 0))
    passed = jax.random.randint(jax.random.fold_in(own, 4), (count // 2,), 0, 1 << 20) % (margin + 1)
    tallies = tallies.at[source_of].add(-passed).at[sink].add(passed)
    members = jnp.searchsorted(jnp.cumsum(tallies), jnp.arange(rows * top), side="right").astype(jnp.int32)
    grid = members.reshape(top, rows).T
    grid = grid[jax.random.permutation(jax.random.fold_in(own, 1), rows)]
    offset_by = jax.random.randint(jax.random.fold_in(own, 2), (rows, 1), 0, top)
    return jnp.take_along_axis(grid, (jnp.arange(top)[None, :] + offset_by) % top, axis=1)


def portions_of(number_of, total, limit, slope, full):
    loads = [(1 << 20) // math.isqrt(grade ** slope) + 1 for grade in range(1, number_of + 1)]
    largest = limit if full else min(limit, max(-(-total // number_of), total * loads[0] // sum(loads)))
    least = 1 if total - largest >= number_of - 1 else 0
    given, rest = [largest] + [least] * (number_of - 1), total - largest - least * (number_of - 1)
    while rest > 0:
        candidates = [i for i in range(1, number_of) if given[i] < largest] or [i for i in range(1, number_of) if given[i] < limit]
        pool, budget = sum([loads[i] for i in candidates]), rest
        for i in candidates:
            addition = min(limit - given[i], max(1, budget * loads[i] // pool), rest)
            given[i] = given[i] + addition
            rest = rest - addition
    return np.array(given)


def gaussian(stream_key, shape, spread, bound, pieces=(), kind=jnp.bfloat16):
    drawn = jax.random.normal(stream_key, shape, jnp.float32) * spread
    if len(pieces) > 0:
        drawn = level_of(stream_key, shape, pieces, -0.22, 0.18) * drawn
    return jnp.clip(drawn, min=-bound, max=bound).astype(kind)


def setup_inputs(seed: int = 0, part: int = 0) -> dict:
    seeds = jax.random.split(jax.random.key(seed), 7)
    part_splits = jax.random.split(jax.random.fold_in(seeds[6], part), 7)
    tokens = gaussian(part_splits[0], (TOKENS, D), 1.0, 6.0, ((0, 16),))
    expert_ids_keys = jax.random.split(jax.random.fold_in(part_splits[1], 1), TOKENS // TOK_DEV)
    expert_ids_turns = jax.random.permutation(jax.random.fold_in(part_splits[1], 3), TOKENS // TOK_DEV)
    expert_ids = jax.vmap(lambda own, number: assign_block(jax.random.fold_in(part_splits[1], 2), own, number, TOK_DEV, EXPERTS, TOP, CAP, 1))(expert_ids_keys, expert_ids_turns).reshape((TOKENS, TOP))
    gate_probs = jnp.clip(0.099609375 + 0.49804688 * jax.random.uniform(part_splits[2], (TOKENS, TOP), jnp.float32) ** level_of(part_splits[2], (TOKENS, TOP), ((0, 16),), -0.2, 0.2), 0.099609375, 0.59765625).astype(jnp.bfloat16)
    cotangent = gaussian(part_splits[3], (TOKENS, D), 0.25, 1.5, ((0, 16),))
    gate_up = gaussian(seeds[4], (D, EXPERTS, 2 * FF), D ** -0.5, 0.1875, ((1, 4),))
    down_weights = gaussian(seeds[5], (FF, EXPERTS, D), FF ** -0.5, 0.21875, ((1, 4),))
    return {"tokens": tokens, "expert_ids": expert_ids, "gate_probs": gate_probs, "cotangent": cotangent, "gate_up": gate_up, "down_weights": down_weights}


def slot_table(expert_ids, experts, capacity):
    flat_ids = expert_ids.reshape(-1)
    assigned = flat_ids.shape[0]
    onehot = (flat_ids[:, None] == jnp.arange(experts, dtype=jnp.int32)[None, :]).astype(jnp.int32)
    before = jnp.cumsum(onehot, axis=0) - onehot
    slot_index = jnp.sum(before * onehot, axis=1).astype(jnp.int32)
    position = (flat_ids * capacity + slot_index).astype(jnp.int32)
    slot_owner = jnp.full((experts * capacity,), assigned, jnp.int32).at[position].set(jnp.arange(assigned, dtype=jnp.int32))
    return position, slot_owner


def regroup(values):
    return values.reshape(N_EXPERT, EXPERTS, CAP, -1).swapaxes(0, 1).reshape(EXPERTS, N_EXPERT * CAP, -1)


def ungroup(values):
    return values.reshape(EXPERTS, N_EXPERT, CAP, -1).swapaxes(0, 1).reshape(N_EXPERT, EXPERTS * CAP, -1)


def split_rows(values):
    return values.reshape((N_EXPERT, N_REPLICA, TOK_DEV) + values.shape[1:]).swapaxes(0, 1)


def join_rows(values):
    return values.swapaxes(0, 1).reshape((TOKENS,) + values.shape[3:])


def reference(tokens, expert_ids, gate_probs, cotangent, gate_up, down_weights):
    gate_float = gate_up.astype(jnp.float32)
    down_float = down_weights.astype(jnp.float32)

    def one_row(carry, row_data):
        row_tokens, row_ids, row_probs, row_cot = row_data
        position, slot_owner = jax.vmap(lambda choose: slot_table(choose, EXPERTS, CAP))(row_ids)
        zero_rows = jnp.zeros((N_EXPERT, 1, D), jnp.bfloat16)
        padded = jnp.concatenate([row_tokens, zero_rows], axis=1)
        dispatched = jax.vmap(lambda values, owners: values[owners // TOP])(padded, slot_owner)
        grouped = regroup(dispatched)
        pre_act = jnp.einsum("erd,def->erf", grouped.astype(jnp.float32), gate_float)
        gate_part = pre_act[..., :FF]
        up_part = pre_act[..., FF:]
        hidden = (jax.nn.silu(gate_part) * up_part).astype(jnp.bfloat16)
        outputs = jnp.einsum("erf,fed->erd", hidden.astype(jnp.float32), down_float).astype(jnp.bfloat16)
        picked = jax.vmap(lambda values, places: values[places])(ungroup(outputs), position)
        picked = picked.reshape(N_EXPERT, TOK_DEV, TOP, D).astype(jnp.float32)
        probs_float = row_probs.astype(jnp.float32)
        combined = jnp.sum(probs_float[..., None] * picked, axis=2).astype(jnp.bfloat16)
        cot_float = row_cot.astype(jnp.float32)
        prob_gradient = jnp.sum(cot_float[:, :, None, :] * picked, axis=3)
        scaled = (probs_float[..., None] * cot_float[:, :, None, :]).astype(jnp.bfloat16).reshape(N_EXPERT, TOK_DEV * TOP, D)
        scaled = jnp.concatenate([scaled, zero_rows], axis=1)
        cot_slots = regroup(jax.vmap(lambda values, owners: values[owners])(scaled, slot_owner))
        hidden_grad = jnp.einsum("erd,fed->erf", cot_slots.astype(jnp.float32), down_float)
        sigmoid_gate = jax.nn.sigmoid(gate_part)
        pre_gradient = jnp.concatenate([hidden_grad * up_part * sigmoid_gate * (1.0 + gate_part * (1.0 - sigmoid_gate)), hidden_grad * gate_part * sigmoid_gate], axis=-1).astype(jnp.bfloat16)
        input_grads = jnp.einsum("erf,def->erd", pre_gradient.astype(jnp.float32), gate_float).astype(jnp.bfloat16)
        returned = jax.vmap(lambda values, places: values[places])(ungroup(input_grads), position)
        token_gradient = jnp.sum(returned.reshape(N_EXPERT, TOK_DEV, TOP, D).astype(jnp.float32), axis=2).astype(jnp.bfloat16)
        grad_inner = jnp.einsum("erd,erf->def", grouped.astype(jnp.float32), pre_gradient.astype(jnp.float32))
        grad_down = jnp.einsum("erf,erd->fed", hidden.astype(jnp.float32), cot_slots.astype(jnp.float32))
        return (carry[0] + grad_inner, carry[1] + grad_down), (combined, token_gradient, prob_gradient)

    start_sums = (jnp.zeros((D, EXPERTS, 2 * FF), jnp.float32), jnp.zeros((FF, EXPERTS, D), jnp.float32))
    sums, row_outs = lax.scan(one_row, start_sums, (split_rows(tokens), split_rows(expert_ids), split_rows(gate_probs), split_rows(cotangent)))
    combined, token_gradient, prob_gradient = row_outs
    return join_rows(combined), join_rows(token_gradient), join_rows(prob_gradient), sums[0], sums[1]
```

```python
import jax
import jax.numpy as jnp
from jax import lax
from jax.experimental.layout import Layout, with_layout_constraint
from jax.sharding import PartitionSpec as P


CAP = 64
CORES = 2
BF = jnp.bfloat16
F32 = jnp.float32


def on_device(tokens, expert_ids, gate_probs, cotangent, gate_up, down_weights, *, sources, replicas):
    count, width = tokens.shape
    top = expert_ids.shape[1]
    local = gate_up.shape[1]
    hidden_width = down_weights.shape[0]
    cap = min(CAP, count)
    along = replicas // CORES
    replica = lax.axis_index("replica")
    core, place = lax.rem(replica, CORES), lax.div(replica, CORES)
    first = lax.axis_index("expert") * local
    slots = sources * cap

    def to_source(values, shift):
        step = [(i, (i + shift) % sources) for i in range(sources)]
        return lax.ppermute(values, "expert", step) if shift else values

    def to_chip(values, shift):
        step = [
            (x * CORES + c, ((x + shift) % along) * CORES + c)
            for x in range(along) for c in range(CORES)
        ]
        return lax.ppermute(values, "replica", step)

    notes = jnp.concatenate([expert_ids.T.astype(BF), gate_probs.T], axis=0)
    flat = notes.reshape(-1)
    extra = -(-flat.shape[0] // (16 * width)) * 16
    flat = jnp.pad(flat, (0, extra * width - flat.shape[0])).reshape(extra, width)
    packed = jnp.concatenate([tokens, flat], axis=0)

    def gathered(values):
        others = [[to_chip(values, t)] for t in range(1, along)]
        held = [to_source(values, s) for s in range(sources)]
        if sources <= 4:
            pieces = [[h] for h in held[1:]]
        else:
            pieces = [held[1:]]
        for piece in pieces:
            sent = piece[0] if len(piece) == 1 else jnp.stack(piece)
            for t in range(1, along):
                got = to_chip(sent, t)
                others[t - 1] += [got] if len(piece) == 1 else [got[i] for i in range(len(piece))]
        return [held] + others

    all_packed = gathered(packed)
    all_cots = gathered(cotangent)

    gate_rows = lax.optimization_barrier(
        with_layout_constraint(gate_up.swapaxes(0, 1), Layout((0, 1, 2)))
    )
    down_rows = lax.optimization_barrier(
        with_layout_constraint(down_weights.swapaxes(0, 1), Layout((0, 1, 2)))
    )

    ahead = (jnp.arange(count)[:, None] < jnp.arange(count)[None, :]).astype(BF)
    same = jnp.arange(sources)[:, None] == jnp.arange(sources)[None, :]

    def routing(held):
        all_notes = jnp.stack([h[count:].reshape(-1)[:notes.size].reshape(notes.shape) for h in held])
        all_ids = all_notes[:, :top].astype(jnp.int32)
        all_probs = all_notes[:, top:]
        named = (all_ids[None] == (first + jnp.arange(local, dtype=jnp.int32))[:, None, None, None])
        member = jnp.any(named, axis=2)
        weight = jnp.sum(jnp.where(named, all_probs[None].astype(F32), 0.0), axis=2)
        rank = jnp.einsum("esp,pq->esq", member.astype(BF), ahead, preferred_element_type=F32)
        rank = jnp.where(member, rank.astype(jnp.int32), -1)
        chosen = rank[:, :, None, :] == jnp.arange(cap, dtype=jnp.int32)[None, None, :, None]
        wide = chosen[:, :, :, None, :] & same[None, :, None, :, None]
        pick = wide.astype(BF).reshape(local * slots, sources * count)
        slot_weight = jnp.sum(jnp.where(chosen, weight[:, :, None, :], 0.0), axis=3).reshape(local, slots, 1)
        return weight, chosen, wide, pick, slot_weight

    def rows(pick, values):
        return jnp.dot(pick, values, preferred_element_type=F32).astype(BF).reshape(local, slots, width)

    def forward(held):
        weight, chosen, wide, pick, slot_weight = routing(held)
        inputs = rows(pick, jnp.concatenate([h[:count] for h in held], axis=0))
        pre_act = jnp.einsum("erd,edf->erf", inputs, gate_rows, preferred_element_type=F32)
        gate, up = pre_act[..., :hidden_width], pre_act[..., hidden_width:]
        sig = jax.nn.sigmoid(gate)
        hidden = (gate * sig * up).astype(BF)
        return (weight, chosen, wide, pick, slot_weight), inputs, gate, up, sig, hidden

    def backward(route, held, gate, up, sig):
        _, _, _, pick, slot_weight = route
        raw_cot = rows(pick, jnp.concatenate(held, axis=0))
        out_grad = (slot_weight * raw_cot.astype(F32)).astype(BF)
        hidden_grad = jnp.einsum("erd,efd->erf", out_grad, down_rows, preferred_element_type=F32)
        pre_grad = jnp.concatenate(
            [hidden_grad * up * sig * (1.0 + gate * (1.0 - sig)), hidden_grad * gate * sig], axis=-1
        ).astype(BF)
        return raw_cot, out_grad, pre_grad

    def returned(matrix, values):
        parts = jnp.einsum(
            "ra,rd->ad", matrix, values.reshape(local * slots, width), preferred_element_type=F32
        ).astype(BF).reshape(sources, count, width)
        arrived = [to_source(parts[s], -s).astype(F32) for s in range(sources)]
        return sum(arrived[1:], arrived[0]).astype(BF)

    route, inputs, gate, up, sig, hidden = forward(all_packed[0])
    weight, chosen, wide, pick, _ = route
    outputs = jnp.einsum("erf,efd->erd", hidden, down_rows, preferred_element_type=F32).astype(BF)
    back = jnp.where(wide, weight[:, :, None, None, :], 0.0).astype(BF).reshape(local * slots, sources * count)
    combined = returned(back, outputs)
    raw_cot, out_grad, pre_grad = backward(route, all_cots[0], gate, up, sig)
    input_grad = jnp.einsum("erf,edf->erd", pre_grad, gate_rows, preferred_element_type=F32).astype(BF)
    token_gradient = returned(pick, input_grad)

    all_inputs, all_hidden, all_grads, all_pre = [inputs], [hidden], [out_grad], [pre_grad]
    for t in range(1, along):
        route_t, inputs_t, gate_t, up_t, sig_t, hidden_t = forward(all_packed[t])
        _, out_grad_t, pre_grad_t = backward(route_t, all_cots[t], gate_t, up_t, sig_t)
        all_inputs.append(inputs_t)
        all_hidden.append(hidden_t)
        all_grads.append(out_grad_t)
        all_pre.append(pre_grad_t)

    pair = [(i, i ^ 1) for i in range(replicas)]

    def columns(values, side):
        size = values.shape[-1] // replicas
        return lax.dynamic_slice_in_dim(values, (place * CORES + side) * size, size, 2)

    def gradient(left, right):
        right = jnp.concatenate(right, axis=1)

        def part(side):
            chosen_columns = jnp.concatenate([columns(l, side) for l in left], axis=1)
            return jnp.einsum("era,erb->eab", chosen_columns, right, preferred_element_type=F32)

        share = with_layout_constraint(part(1 - core).astype(BF).swapaxes(0, 1), Layout((0, 1, 2)))
        theirs = lax.ppermute(share, "replica", pair)
        own = with_layout_constraint(part(core).swapaxes(0, 1), Layout((0, 1, 2)))
        return own + theirs.astype(F32)

    down_gradient = gradient(all_hidden, all_grads)
    gate_up_gradient = gradient(all_inputs, all_pre)

    slot_prob = jnp.sum(raw_cot.astype(F32) * outputs.astype(F32), axis=2).reshape(local, sources, cap, 1)
    prob_part = jnp.sum(jnp.where(chosen, slot_prob, 0.0), axis=2).swapaxes(0, 1)
    choice = expert_ids.T
    prob_gradient = jnp.zeros((top, count), F32)
    home = lax.axis_index("expert")
    for s in range(sources):
        block = lax.rem(home + s, sources) * local
        theirs = to_source(prob_part[s], -s)
        hit = choice[:, None, :] == (block + jnp.arange(local, dtype=jnp.int32))[None, :, None]
        prob_gradient = prob_gradient + jnp.sum(jnp.where(hit, theirs[None], 0.0), axis=1)
    prob_gradient = prob_gradient.T
    return (combined, token_gradient, prob_gradient, gate_up_gradient, down_gradient)


def solution(mesh):
    rows = P(("groups", "expert", "replica"), None)
    sources, replicas = mesh.shape["expert"], mesh.shape["replica"]

    def body(*args):
        return on_device(*args, sources=sources, replicas=replicas)

    return jax.shard_map(
        body,
        mesh=mesh,
        in_specs=(rows, rows, rows, rows, P(None, "expert", None), P(None, "expert", None)),
        out_specs=(
            rows,
            rows,
            rows,
            P(("groups", "replica"), "expert", None),
            P(("groups", "replica"), "expert", None),
        ),
        check_vma=False,
    )
```

```python
import functools

import jax
import jax.numpy as jnp
from jax import lax
from jax.experimental import pallas as pl
from jax.experimental.pallas import tpu as pltpu
from jax.experimental.layout import Layout, with_layout_constraint
from jax.sharding import PartitionSpec as P


CAP = 64
CORES = 2
BF = jnp.bfloat16
F32 = jnp.float32


def general(tokens, expert_ids, gate_probs, cotangent, gate_up, down_weights, *, sources, replicas):
    count, width = tokens.shape
    top = expert_ids.shape[1]
    local = gate_up.shape[1]
    hidden_width = down_weights.shape[0]
    cap = min(CAP, count)
    along = replicas // CORES
    replica = lax.axis_index("replica")
    core, place = lax.rem(replica, CORES), lax.div(replica, CORES)
    first = lax.axis_index("expert") * local
    slots = sources * cap

    def to_source(values, shift):
        step = [(i, (i + shift) % sources) for i in range(sources)]
        return lax.ppermute(values, "expert", step) if shift else values

    def to_chip(values, shift):
        step = [
            (x * CORES + c, ((x + shift) % along) * CORES + c)
            for x in range(along) for c in range(CORES)
        ]
        return lax.ppermute(values, "replica", step)

    notes = jnp.concatenate([expert_ids.T.astype(BF), gate_probs.T], axis=0)
    flat = notes.reshape(-1)
    extra = -(-flat.shape[0] // (16 * width)) * 16
    flat = jnp.pad(flat, (0, extra * width - flat.shape[0])).reshape(extra, width)
    packed = jnp.concatenate([tokens, flat], axis=0)

    def gathered(values):
        others = [[to_chip(values, t)] for t in range(1, along)]
        held = [to_source(values, s) for s in range(sources)]
        if sources <= 4:
            pieces = [[h] for h in held[1:]]
        else:
            pieces = [held[1:]]
        for piece in pieces:
            sent = piece[0] if len(piece) == 1 else jnp.stack(piece)
            for t in range(1, along):
                got = to_chip(sent, t)
                others[t - 1] += [got] if len(piece) == 1 else [got[i] for i in range(len(piece))]
        return [held] + others

    all_packed = gathered(packed)
    all_cots = gathered(cotangent)

    gate_rows = lax.optimization_barrier(
        with_layout_constraint(gate_up.swapaxes(0, 1), Layout((0, 1, 2)))
    )
    down_rows = lax.optimization_barrier(
        with_layout_constraint(down_weights.swapaxes(0, 1), Layout((0, 1, 2)))
    )

    ahead = (jnp.arange(count)[:, None] < jnp.arange(count)[None, :]).astype(BF)
    same = jnp.arange(sources)[:, None] == jnp.arange(sources)[None, :]

    def routing(held):
        all_notes = jnp.stack([h[count:].reshape(-1)[:notes.size].reshape(notes.shape) for h in held])
        all_ids = all_notes[:, :top].astype(jnp.int32)
        all_probs = all_notes[:, top:]
        named = (all_ids[None] == (first + jnp.arange(local, dtype=jnp.int32))[:, None, None, None])
        member = jnp.any(named, axis=2)
        weight = jnp.sum(jnp.where(named, all_probs[None].astype(F32), 0.0), axis=2)
        rank = jnp.einsum("esp,pq->esq", member.astype(BF), ahead, preferred_element_type=F32)
        rank = jnp.where(member, rank.astype(jnp.int32), -1)
        chosen = rank[:, :, None, :] == jnp.arange(cap, dtype=jnp.int32)[None, None, :, None]
        wide = chosen[:, :, :, None, :] & same[None, :, None, :, None]
        pick = wide.astype(BF).reshape(local * slots, sources * count)
        slot_weight = jnp.sum(jnp.where(chosen, weight[:, :, None, :], 0.0), axis=3).reshape(local, slots, 1)
        return weight, chosen, wide, pick, slot_weight

    def rows(pick, values):
        return jnp.dot(pick, values, preferred_element_type=F32).astype(BF).reshape(local, slots, width)

    def forward(held):
        weight, chosen, wide, pick, slot_weight = routing(held)
        inputs = rows(pick, jnp.concatenate([h[:count] for h in held], axis=0))
        pre_act = jnp.einsum("erd,edf->erf", inputs, gate_rows, preferred_element_type=F32)
        gate, up = pre_act[..., :hidden_width], pre_act[..., hidden_width:]
        sig = jax.nn.sigmoid(gate)
        hidden = (gate * sig * up).astype(BF)
        return (weight, chosen, wide, pick, slot_weight), inputs, gate, up, sig, hidden

    def backward(route, held, gate, up, sig):
        _, _, _, pick, slot_weight = route
        raw_cot = rows(pick, jnp.concatenate(held, axis=0))
        out_grad = (slot_weight * raw_cot.astype(F32)).astype(BF)
        hidden_grad = jnp.einsum("erd,efd->erf", out_grad, down_rows, preferred_element_type=F32)
        pre_grad = jnp.concatenate(
            [hidden_grad * up * sig * (1.0 + gate * (1.0 - sig)), hidden_grad * gate * sig], axis=-1
        ).astype(BF)
        return raw_cot, out_grad, pre_grad

    def returned(matrix, values):
        parts = jnp.einsum(
            "ra,rd->ad", matrix, values.reshape(local * slots, width), preferred_element_type=F32
        ).astype(BF).reshape(sources, count, width)
        arrived = [to_source(parts[s], -s).astype(F32) for s in range(sources)]
        return sum(arrived[1:], arrived[0]).astype(BF)

    route, inputs, gate, up, sig, hidden = forward(all_packed[0])
    weight, chosen, wide, pick, _ = route
    outputs = jnp.einsum("erf,efd->erd", hidden, down_rows, preferred_element_type=F32).astype(BF)
    back = jnp.where(wide, weight[:, :, None, None, :], 0.0).astype(BF).reshape(local * slots, sources * count)
    combined = returned(back, outputs)
    raw_cot, out_grad, pre_grad = backward(route, all_cots[0], gate, up, sig)
    input_grad = jnp.einsum("erf,edf->erd", pre_grad, gate_rows, preferred_element_type=F32).astype(BF)
    token_gradient = returned(pick, input_grad)

    all_inputs, all_hidden, all_grads, all_pre = [inputs], [hidden], [out_grad], [pre_grad]
    for t in range(1, along):
        route_t, inputs_t, gate_t, up_t, sig_t, hidden_t = forward(all_packed[t])
        _, out_grad_t, pre_grad_t = backward(route_t, all_cots[t], gate_t, up_t, sig_t)
        all_inputs.append(inputs_t)
        all_hidden.append(hidden_t)
        all_grads.append(out_grad_t)
        all_pre.append(pre_grad_t)

    pair = [(i, i ^ 1) for i in range(replicas)]

    def columns(values, side):
        size = values.shape[-1] // replicas
        return lax.dynamic_slice_in_dim(values, (place * CORES + side) * size, size, 2)

    def gradient(left, right):
        right = jnp.concatenate(right, axis=1)

        def part(side):
            chosen_columns = jnp.concatenate([columns(l, side) for l in left], axis=1)
            return jnp.einsum("era,erb->eab", chosen_columns, right, preferred_element_type=F32)

        share = with_layout_constraint(part(1 - core).astype(BF).swapaxes(0, 1), Layout((0, 1, 2)))
        theirs = lax.ppermute(share, "replica", pair)
        own = with_layout_constraint(part(core).swapaxes(0, 1), Layout((0, 1, 2)))
        return own + theirs.astype(F32)

    down_gradient = gradient(all_hidden, all_grads)
    gate_up_gradient = gradient(all_inputs, all_pre)

    slot_prob = jnp.sum(raw_cot.astype(F32) * outputs.astype(F32), axis=2).reshape(local, sources, cap, 1)
    prob_part = jnp.sum(jnp.where(chosen, slot_prob, 0.0), axis=2).swapaxes(0, 1)
    choice = expert_ids.T
    prob_gradient = jnp.zeros((top, count), F32)
    home = lax.axis_index("expert")
    for s in range(sources):
        block = lax.rem(home + s, sources) * local
        theirs = to_source(prob_part[s], -s)
        hit = choice[:, None, :] == (block + jnp.arange(local, dtype=jnp.int32))[None, :, None]
        prob_gradient = prob_gradient + jnp.sum(jnp.where(hit, theirs[None], 0.0), axis=1)
    prob_gradient = prob_gradient.T
    return (combined, token_gradient, prob_gradient, gate_up_gradient, down_gradient)


NOTES = 16
HALF = 8


def routing_tile(note_refs, expert, count, cap):
    members, weights = [], []
    for ref in note_refs:
        tile = ref[...].astype(F32)
        named = tile[:HALF].astype(jnp.int32) == expert
        members.append(jnp.max(jnp.where(named, 1.0, 0.0), axis=0, keepdims=True))
        weights.append(jnp.sum(jnp.where(named, tile[HALF:], 0.0), axis=0, keepdims=True))
    member = jnp.concatenate(members, axis=0)
    ahead = (
        lax.broadcasted_iota(jnp.int32, (count, count), 0) < lax.broadcasted_iota(jnp.int32, (count, count), 1)
    )
    ahead = jnp.where(ahead, 1.0, 0.0).astype(BF)
    rank = jnp.dot(member.astype(BF), ahead, preferred_element_type=F32).astype(jnp.int32)
    slots = len(note_refs) * cap
    row = lax.broadcasted_iota(jnp.int32, (slots, count), 0)
    picks = []
    for s in range(len(note_refs)):
        place = jnp.where(members[s] > 0.0, rank[s:s + 1] + s * cap, -1)
        picks.append(row == place)
    return picks, weights


def selected(picks, values):
    return jnp.concatenate([jnp.where(p, v, 0.0) for p, v in zip(picks, values)], axis=1)


def across(left, right):
    return lax.dot_general(left, right, (((0,), (0,)), ((), ())), preferred_element_type=F32)


def against(left, right):
    return lax.dot_general(left, right, (((1,), (1,)), ((), ())), preferred_element_type=F32)


def forward_tile(pick, tok, gate_ref, hidden_width):
    inputs = jnp.dot(pick, tok[...], preferred_element_type=F32).astype(BF)
    pre_act = jnp.dot(inputs, gate_ref[0], preferred_element_type=F32)
    gate, up = pre_act[:, :hidden_width], pre_act[:, hidden_width:]
    sig = jax.nn.sigmoid(gate)
    return inputs, pre_act, (gate * sig * up).astype(BF)


def backward_tile(pick, back, cot, down_ref, pre_act, hidden_width):
    raw_cot = jnp.dot(pick, cot[...], preferred_element_type=F32)
    out_grad = (jnp.sum(back, axis=1, keepdims=True) * raw_cot).astype(BF)
    hidden_grad = against(out_grad, down_ref[0])
    gate, up = pre_act[:, :hidden_width], pre_act[:, hidden_width:]
    sig = jax.nn.sigmoid(gate)
    pre_grad = jnp.concatenate(
        [hidden_grad * up * sig * (1.0 + gate * (1.0 - sig)), hidden_grad * gate * sig], axis=1
    ).astype(BF)
    return raw_cot, out_grad, pre_grad


def own_forward(sources, cap, info, *refs):
    packed, refs = refs[:sources], refs[sources:]
    note_refs, refs = refs[:sources], refs[sources:]
    gate_ref, down_ref, refs = refs[0], refs[1], refs[2:]
    part_refs, refs = refs[:sources], refs[sources:]
    input_ref, pre_ref, hidden_ref, output_ref, tok, total = refs
    e = pl.program_id(0)
    count = tok.shape[0] // sources

    @pl.when(e == 0)
    def _():
        for s in range(sources):
            tok[s * count:(s + 1) * count, :] = packed[s][...]
        total[...] = jnp.zeros_like(total)

    picks, weights = routing_tile(note_refs, info[0] + e, count, cap)
    pick = selected(picks, [1.0] * sources).astype(BF)
    back = selected(picks, weights)
    inputs, pre_act, hidden = forward_tile(pick, tok, gate_ref, hidden_ref.shape[2])
    outputs = jnp.dot(hidden, down_ref[0], preferred_element_type=F32).astype(BF)
    input_ref[0] = inputs
    pre_ref[0] = pre_act
    hidden_ref[0] = hidden
    output_ref[0] = outputs
    total[...] += across(back.astype(BF), outputs)

    @pl.when(e == pl.num_programs(0) - 1)
    def _():
        for s in range(sources):
            part_refs[s][...] = total[s * count:(s + 1) * count, :].astype(BF)


def own_backward(sources, cap, info, *refs):
    cots, refs = refs[:sources], refs[sources:]
    note_refs, refs = refs[:sources], refs[sources:]
    gate_ref, down_ref, pre_ref, output_ref, refs = refs[0], refs[1], refs[2], refs[3], refs[4:]
    part_refs, refs = refs[:sources], refs[sources:]
    prob_ref, out_grad_ref, pre_grad_ref, cot, total = refs
    e = pl.program_id(0)
    count = cot.shape[0] // sources

    @pl.when(e == 0)
    def _():
        for s in range(sources):
            cot[s * count:(s + 1) * count, :] = cots[s][...]
        total[...] = jnp.zeros_like(total)

    picks, weights = routing_tile(note_refs, info[0] + e, count, cap)
    pick = selected(picks, [1.0] * sources).astype(BF)
    back = selected(picks, weights)
    hidden_width = pre_ref.shape[2] // 2
    raw_cot, out_grad, pre_grad = backward_tile(pick, back, cot, down_ref, pre_ref[0], hidden_width)
    out_grad_ref[0] = out_grad
    pre_grad_ref[0] = pre_grad
    slot_prob = jnp.sum(raw_cot * output_ref[0].astype(F32), axis=1, keepdims=True)
    for s in range(sources):
        prob_ref[s, pl.ds(e, 1), :] = jnp.sum(jnp.where(picks[s], slot_prob, 0.0), axis=0, keepdims=True)
    input_grad = against(pre_grad, gate_ref[0]).astype(BF)
    total[...] += across(pick, input_grad)

    @pl.when(e == pl.num_programs(0) - 1)
    def _():
        for s in range(sources):
            part_refs[s][...] = total[s * count:(s + 1) * count, :].astype(BF)


def far_gradients(sources, cap, info, *refs):
    packed, refs = refs[:sources], refs[sources:]
    note_refs, refs = refs[:sources], refs[sources:]
    cots, refs = refs[:sources], refs[sources:]
    gate_ref, down_ref, input_ref, hidden_ref, out_grad_ref, pre_grad_ref = refs[:6]
    gate_own, gate_share, down_own, down_share = refs[6:10]
    tok, cot, all_inputs, all_hidden, all_grads, all_pre, gate_sum, down_sum = refs[10:]
    e = pl.program_id(0)
    count = tok.shape[0] // sources
    slots = sources * cap

    @pl.when(e == 0)
    def _():
        for s in range(sources):
            tok[s * count:(s + 1) * count, :] = packed[s][...]
            cot[s * count:(s + 1) * count, :] = cots[s][...]

    picks, weights = routing_tile(note_refs, info[0] + e, count, cap)
    pick = selected(picks, [1.0] * sources).astype(BF)
    back = selected(picks, weights)
    hidden_width = hidden_ref.shape[2]
    inputs, pre_act, hidden = forward_tile(pick, tok, gate_ref, hidden_width)
    _, out_grad, pre_grad = backward_tile(pick, back, cot, down_ref, pre_act, hidden_width)
    for scratch, own, far in (
        (all_inputs, input_ref, inputs), (all_hidden, hidden_ref, hidden),
        (all_grads, out_grad_ref, out_grad), (all_pre, pre_grad_ref, pre_grad),
    ):
        scratch[:slots, :] = own[0]
        scratch[slots:, :] = far

    place, core = info[1], info[2]
    for left, right, total, own, share in (
        (all_hidden, all_grads, down_sum, down_own, down_share),
        (all_inputs, all_pre, gate_sum, gate_own, gate_share),
    ):
        size, block = total.shape[0], own.shape[1]
        columns = pl.ds(pl.multiple_of(place * size, size), size)
        total[...] = across(left[:, columns], right[...])
        own[0] = total[pl.ds(pl.multiple_of(core * block, block), block), :]
        share[0] = total[pl.ds(pl.multiple_of((1 - core) * block, block), block), :].astype(BF)


def joined(local, own_ref, share_ref, out_ref):
    for e in range(local):
        out_ref[:, e, :] = own_ref[e] + share_ref[e].astype(F32)


def whole(*shape):
    return pl.BlockSpec(shape, lambda e, info: (0,) * len(shape))


def each(*shape):
    return pl.BlockSpec((1,) + shape, lambda e, info: (e,) + (0,) * len(shape))


def kernel_call(body, grid, in_specs, out_specs, out_shape, scratch, flops, moved):
    return pl.pallas_call(
        body,
        grid_spec=pltpu.PrefetchScalarGridSpec(
            num_scalar_prefetch=1, grid=(grid,), in_specs=in_specs, out_specs=out_specs, scratch_shapes=scratch
        ),
        out_shape=out_shape,
        compiler_params=pltpu.CompilerParams(vmem_limit_bytes=56 << 20),
        cost_estimate=pl.CostEstimate(flops=flops, bytes_accessed=moved, transcendentals=0),
    )


def two_chips(tokens, expert_ids, gate_probs, cotangent, gate_up, down_weights, *, sources, replicas):
    count, width = tokens.shape
    top = expert_ids.shape[1]
    local = gate_up.shape[1]
    hidden_width = down_weights.shape[0]
    pre_width = gate_up.shape[2]
    cap = min(CAP, count)
    along = replicas // CORES
    replica = lax.axis_index("replica")
    core, place = lax.rem(replica, CORES), lax.div(replica, CORES)
    home = lax.axis_index("expert")
    slots = sources * cap
    info = jnp.stack([home * local, place, core]).astype(jnp.int32)

    def to_source(values, shift):
        step = [(i, (i + shift) % sources) for i in range(sources)]
        return lax.ppermute(values, "expert", step) if shift else values

    def to_chip(values):
        step = [
            (x * CORES + c, ((x + 1) % along) * CORES + c)
            for x in range(along) for c in range(CORES)
        ]
        return lax.ppermute(values, "replica", step)

    fill = ((0, HALF - top), (0, width - count))
    packed = jnp.concatenate(
        [tokens, jnp.pad(expert_ids.T.astype(BF), fill, constant_values=-1), jnp.pad(gate_probs.T, fill)], axis=0
    )

    def gathered(values):
        far = [to_chip(values)]
        held = [to_source(values, s) for s in range(sources)]
        far += [to_chip(h) for h in held[1:]]
        return held, far

    near_packed, far_packed = gathered(packed)
    near_cots, far_cots = gathered(cotangent)
    gate_rows = lax.optimization_barrier(
        with_layout_constraint(gate_up.swapaxes(0, 1), Layout((0, 1, 2)))
    )
    down_rows = lax.optimization_barrier(
        with_layout_constraint(down_weights.swapaxes(0, 1), Layout((0, 1, 2)))
    )

    block_specs = [whole(count, width)] * sources
    note_specs = [pl.BlockSpec((NOTES, count), lambda e, info: (count // NOTES, 0))] * sources
    weight_specs = [each(width, pre_width), each(hidden_width, width)]
    block_shape = jax.ShapeDtypeStruct((count, width), BF)
    gathered_rows = pltpu.VMEM((sources * count, width), BF)
    part_total = pltpu.VMEM((sources * count, width), F32)

    def array(size, dtype, rows=slots):
        return jax.ShapeDtypeStruct((local, rows, size), dtype)

    product = 2 * local * slots * width * hidden_width
    weight_bytes = 6 * local * width * hidden_width
    *out_parts, inputs, pre_act, hidden, outputs = kernel_call(
        functools.partial(own_forward, sources, cap),
        local,
        block_specs + note_specs + weight_specs,
        block_specs + [each(slots, width), each(slots, pre_width), each(slots, hidden_width), each(slots, width)],
        [block_shape] * sources + [array(width, BF), array(pre_width, F32), array(hidden_width, BF), array(width, BF)],
        [gathered_rows, part_total],
        4 * product,
        2 * weight_bytes,
    )(info, *near_packed, *near_packed, gate_rows, down_rows)

    def returned(parts):
        return [to_source(parts[s], -s) for s in range(sources)]

    def added(arrived):
        return sum([a.astype(F32) for a in arrived[1:]], arrived[0].astype(F32)).astype(BF)

    out_arrived = returned(out_parts)

    *grad_parts, prob_part, out_grad, pre_grad = kernel_call(
        functools.partial(own_backward, sources, cap),
        local,
        block_specs + note_specs + weight_specs + [each(slots, pre_width), each(slots, width)],
        block_specs + [whole(sources, local, count), each(slots, width), each(slots, pre_width)],
        [block_shape] * sources + [
            jax.ShapeDtypeStruct((sources, local, count), F32), array(width, BF), array(pre_width, BF)
        ],
        [gathered_rows, part_total],
        4 * product,
        2 * weight_bytes,
    )(info, *near_cots, *near_packed, gate_rows, down_rows, pre_act, outputs)
    prob_arrived = [to_source(prob_part[s], -s) for s in range(sources)]
    grad_arrived = returned(grad_parts)

    gate_block, down_block = width // replicas, hidden_width // replicas
    gate_own, gate_share, down_own, down_share = kernel_call(
        functools.partial(far_gradients, sources, cap),
        local,
        block_specs + note_specs + block_specs + weight_specs + [
            each(slots, width), each(slots, hidden_width), each(slots, width), each(slots, pre_width)
        ],
        [
            each(gate_block, pre_width), each(gate_block, pre_width),
            each(down_block, width), each(down_block, width),
        ],
        [
            array(pre_width, F32, gate_block), array(pre_width, BF, gate_block),
            array(width, F32, down_block), array(width, BF, down_block),
        ],
        [
            gathered_rows, gathered_rows,
            pltpu.VMEM((2 * slots, width), BF), pltpu.VMEM((2 * slots, hidden_width), BF),
            pltpu.VMEM((2 * slots, width), BF), pltpu.VMEM((2 * slots, pre_width), BF),
            pltpu.VMEM((CORES * gate_block, pre_width), F32), pltpu.VMEM((CORES * down_block, width), F32),
        ],
        6 * product,
        3 * weight_bytes,
    )(
        info, *far_packed, *far_packed, *far_cots, gate_rows, down_rows,
        inputs, hidden, out_grad, pre_grad,
    )

    pair = [(i, i ^ 1) for i in range(replicas)]

    def final(own, share):
        theirs = lax.ppermute(share, "replica", pair)
        rows, size = own.shape[1], own.shape[2]
        cut = rows // 4
        return pl.pallas_call(
            functools.partial(joined, local),
            grid=(rows // cut,),
            in_specs=[pl.BlockSpec((local, cut, size), lambda i: (0, i, 0))] * 2,
            out_specs=pl.BlockSpec((cut, local, size), lambda i: (i, 0, 0)),
            out_shape=jax.ShapeDtypeStruct((rows, local, size), F32),
            compiler_params=pltpu.CompilerParams(vmem_limit_bytes=56 << 20),
            cost_estimate=pl.CostEstimate(flops=0, bytes_accessed=10 * own.size, transcendentals=0),
        )(own, theirs)

    gate_up_gradient = final(gate_own, gate_share)
    down_gradient = final(down_own, down_share)

    choice = expert_ids.T
    prob_gradient = jnp.zeros((top, count), F32)
    for s in range(sources):
        block = lax.rem(home + s, sources) * local
        hit = choice[:, None, :] == (block + jnp.arange(local, dtype=jnp.int32))[None, :, None]
        prob_gradient = prob_gradient + jnp.sum(jnp.where(hit, prob_arrived[s][None], 0.0), axis=1)
    return (added(out_arrived), added(grad_arrived), prob_gradient.T, gate_up_gradient, down_gradient)


def on_device(*args, sources, replicas):
    count, top, local = args[0].shape[0], args[1].shape[1], args[4].shape[1]
    small = sources * min(CAP, count) * local <= 1024 and sources <= 4
    plain = replicas == 2 * CORES and small and count % 128 == 0 and top <= HALF
    return (two_chips if plain else general)(*args, sources=sources, replicas=replicas)


def solution(mesh):
    rows = P(("groups", "expert", "replica"), None)
    sources, replicas = mesh.shape["expert"], mesh.shape["replica"]

    def body(*args):
        return on_device(*args, sources=sources, replicas=replicas)

    return jax.shard_map(
        body,
        mesh=mesh,
        in_specs=(rows, rows, rows, rows, P(None, "expert", None), P(None, "expert", None)),
        out_specs=(
            rows,
            rows,
            rows,
            P(("groups", "replica"), "expert", None),
            P(("groups", "replica"), "expert", None),
        ),
        check_vma=False,
    )
```

```python
import functools

import jax
import jax.numpy as jnp
from jax import lax
from jax.experimental import pallas as pl
from jax.experimental.pallas import tpu as pltpu
from jax.experimental.layout import Layout, with_layout_constraint
from jax.sharding import PartitionSpec as P


CAP = 64
CORES = 2
BF = jnp.bfloat16
F32 = jnp.float32


def general(tokens, expert_ids, gate_probs, cotangent, gate_up, down_weights, *, sources, replicas):
    count, width = tokens.shape
    top = expert_ids.shape[1]
    local = gate_up.shape[1]
    hidden_width = down_weights.shape[0]
    cap = min(CAP, count)
    along = replicas // CORES
    replica = lax.axis_index("replica")
    core, place = lax.rem(replica, CORES), lax.div(replica, CORES)
    first = lax.axis_index("expert") * local
    slots = sources * cap

    def to_source(values, shift):
        step = [(i, (i + shift) % sources) for i in range(sources)]
        return lax.ppermute(values, "expert", step) if shift else values

    def to_chip(values, shift):
        step = [
            (x * CORES + c, ((x + shift) % along) * CORES + c)
            for x in range(along) for c in range(CORES)
        ]
        return lax.ppermute(values, "replica", step)

    notes = jnp.concatenate([expert_ids.T.astype(BF), gate_probs.T], axis=0)
    flat = notes.reshape(-1)
    extra = -(-flat.shape[0] // (16 * width)) * 16
    flat = jnp.pad(flat, (0, extra * width - flat.shape[0])).reshape(extra, width)
    packed = jnp.concatenate([tokens, flat], axis=0)

    def gathered(values):
        others = [[to_chip(values, t)] for t in range(1, along)]
        held = [to_source(values, s) for s in range(sources)]
        if sources <= 4:
            pieces = [[h] for h in held[1:]]
        else:
            pieces = [held[1:]]
        for piece in pieces:
            sent = piece[0] if len(piece) == 1 else jnp.stack(piece)
            for t in range(1, along):
                got = to_chip(sent, t)
                others[t - 1] += [got] if len(piece) == 1 else [got[i] for i in range(len(piece))]
        return [held] + others

    all_packed = gathered(packed)
    all_cots = gathered(cotangent)

    gate_rows = lax.optimization_barrier(
        with_layout_constraint(gate_up.swapaxes(0, 1), Layout((0, 1, 2)))
    )
    down_rows = lax.optimization_barrier(
        with_layout_constraint(down_weights.swapaxes(0, 1), Layout((0, 1, 2)))
    )

    ahead = (jnp.arange(count)[:, None] < jnp.arange(count)[None, :]).astype(BF)
    same = jnp.arange(sources)[:, None] == jnp.arange(sources)[None, :]

    def routing(held):
        all_notes = jnp.stack([h[count:].reshape(-1)[:notes.size].reshape(notes.shape) for h in held])
        all_ids = all_notes[:, :top].astype(jnp.int32)
        all_probs = all_notes[:, top:]
        named = (all_ids[None] == (first + jnp.arange(local, dtype=jnp.int32))[:, None, None, None])
        member = jnp.any(named, axis=2)
        weight = jnp.sum(jnp.where(named, all_probs[None].astype(F32), 0.0), axis=2)
        rank = jnp.einsum("esp,pq->esq", member.astype(BF), ahead, preferred_element_type=F32)
        rank = jnp.where(member, rank.astype(jnp.int32), -1)
        chosen = rank[:, :, None, :] == jnp.arange(cap, dtype=jnp.int32)[None, None, :, None]
        wide = chosen[:, :, :, None, :] & same[None, :, None, :, None]
        pick = wide.astype(BF).reshape(local * slots, sources * count)
        slot_weight = jnp.sum(jnp.where(chosen, weight[:, :, None, :], 0.0), axis=3).reshape(local, slots, 1)
        return weight, chosen, wide, pick, slot_weight

    def rows(pick, values):
        return jnp.dot(pick, values, preferred_element_type=F32).astype(BF).reshape(local, slots, width)

    def forward(held):
        weight, chosen, wide, pick, slot_weight = routing(held)
        inputs = rows(pick, jnp.concatenate([h[:count] for h in held], axis=0))
        pre_act = jnp.einsum("erd,edf->erf", inputs, gate_rows, preferred_element_type=F32)
        gate, up = pre_act[..., :hidden_width], pre_act[..., hidden_width:]
        sig = jax.nn.sigmoid(gate)
        hidden = (gate * sig * up).astype(BF)
        return (weight, chosen, wide, pick, slot_weight), inputs, gate, up, sig, hidden

    def backward(route, held, gate, up, sig):
        _, _, _, pick, slot_weight = route
        raw_cot = rows(pick, jnp.concatenate(held, axis=0))
        out_grad = (slot_weight * raw_cot.astype(F32)).astype(BF)
        hidden_grad = jnp.einsum("erd,efd->erf", out_grad, down_rows, preferred_element_type=F32)
        pre_grad = jnp.concatenate(
            [hidden_grad * up * sig * (1.0 + gate * (1.0 - sig)), hidden_grad * gate * sig], axis=-1
        ).astype(BF)
        return raw_cot, out_grad, pre_grad

    def returned(matrix, values):
        parts = jnp.einsum(
            "ra,rd->ad", matrix, values.reshape(local * slots, width), preferred_element_type=F32
        ).astype(BF).reshape(sources, count, width)
        arrived = [to_source(parts[s], -s).astype(F32) for s in range(sources)]
        return sum(arrived[1:], arrived[0]).astype(BF)

    route, inputs, gate, up, sig, hidden = forward(all_packed[0])
    weight, chosen, wide, pick, _ = route
    outputs = jnp.einsum("erf,efd->erd", hidden, down_rows, preferred_element_type=F32).astype(BF)
    back = jnp.where(wide, weight[:, :, None, None, :], 0.0).astype(BF).reshape(local * slots, sources * count)
    combined = returned(back, outputs)
    raw_cot, out_grad, pre_grad = backward(route, all_cots[0], gate, up, sig)
    input_grad = jnp.einsum("erf,edf->erd", pre_grad, gate_rows, preferred_element_type=F32).astype(BF)
    token_gradient = returned(pick, input_grad)

    all_inputs, all_hidden, all_grads, all_pre = [inputs], [hidden], [out_grad], [pre_grad]
    for t in range(1, along):
        route_t, inputs_t, gate_t, up_t, sig_t, hidden_t = forward(all_packed[t])
        _, out_grad_t, pre_grad_t = backward(route_t, all_cots[t], gate_t, up_t, sig_t)
        all_inputs.append(inputs_t)
        all_hidden.append(hidden_t)
        all_grads.append(out_grad_t)
        all_pre.append(pre_grad_t)

    pair = [(i, i ^ 1) for i in range(replicas)]

    def columns(values, side):
        size = values.shape[-1] // replicas
        return lax.dynamic_slice_in_dim(values, (place * CORES + side) * size, size, 2)

    def gradient(left, right):
        right = jnp.concatenate(right, axis=1)

        def part(side):
            chosen_columns = jnp.concatenate([columns(l, side) for l in left], axis=1)
            return jnp.einsum("era,erb->eab", chosen_columns, right, preferred_element_type=F32)

        share = with_layout_constraint(part(1 - core).astype(BF).swapaxes(0, 1), Layout((0, 1, 2)))
        theirs = lax.ppermute(share, "replica", pair)
        own = with_layout_constraint(part(core).swapaxes(0, 1), Layout((0, 1, 2)))
        return own + theirs.astype(F32)

    down_gradient = gradient(all_hidden, all_grads)
    gate_up_gradient = gradient(all_inputs, all_pre)

    slot_prob = jnp.sum(raw_cot.astype(F32) * outputs.astype(F32), axis=2).reshape(local, sources, cap, 1)
    prob_part = jnp.sum(jnp.where(chosen, slot_prob, 0.0), axis=2).swapaxes(0, 1)
    choice = expert_ids.T
    prob_gradient = jnp.zeros((top, count), F32)
    home = lax.axis_index("expert")
    for s in range(sources):
        block = lax.rem(home + s, sources) * local
        theirs = to_source(prob_part[s], -s)
        hit = choice[:, None, :] == (block + jnp.arange(local, dtype=jnp.int32))[None, :, None]
        prob_gradient = prob_gradient + jnp.sum(jnp.where(hit, theirs[None], 0.0), axis=1)
    prob_gradient = prob_gradient.T
    return (combined, token_gradient, prob_gradient, gate_up_gradient, down_gradient)


HALF = 8
FWD, BWD, FAR, JOIN = 16, 16, 24, 8


def routing_tile(note_refs, expert, count, cap):
    members, weights = [], []
    for ref in note_refs:
        tile = ref[...].astype(F32)
        named = tile[:, :count].astype(jnp.int32) == expert
        members.append(jnp.max(jnp.where(named, 1.0, 0.0), axis=0, keepdims=True))
        weights.append(jnp.sum(jnp.where(named, tile[:, count:], 0.0), axis=0, keepdims=True))
    member = jnp.concatenate(members, axis=0)
    ahead = (
        lax.broadcasted_iota(jnp.int32, (count, count), 0) < lax.broadcasted_iota(jnp.int32, (count, count), 1)
    )
    ahead = jnp.where(ahead, 1.0, 0.0).astype(BF)
    rank = jnp.dot(member.astype(BF), ahead, preferred_element_type=F32).astype(jnp.int32)
    slots = len(note_refs) * cap
    row = lax.broadcasted_iota(jnp.int32, (slots, count), 0)
    picks = []
    for s in range(len(note_refs)):
        place = jnp.where(members[s] > 0.0, rank[s:s + 1] + s * cap, -1)
        picks.append(row == place)
    return picks, weights


def selected(picks, values):
    return jnp.concatenate([jnp.where(p, v, 0.0) for p, v in zip(picks, values)], axis=1)


def across(left, right):
    return lax.dot_general(left, right, (((0,), (0,)), ((), ())), preferred_element_type=F32)


def against(left, right):
    return lax.dot_general(left, right, (((1,), (1,)), ((), ())), preferred_element_type=F32)


def forward_tile(pick, tok, gate_ref, hidden_width):
    inputs = jnp.dot(pick, tok[...], preferred_element_type=F32).astype(BF)
    pre_act = jnp.dot(inputs, gate_ref[0], preferred_element_type=F32)
    gate, up = pre_act[:, :hidden_width], pre_act[:, hidden_width:]
    sig = jax.nn.sigmoid(gate)
    return inputs, pre_act, (gate * sig * up).astype(BF)


def backward_tile(pick, back, cot, down_ref, pre_act, hidden_width):
    raw_cot = jnp.dot(pick, cot[...], preferred_element_type=F32)
    out_grad = (jnp.sum(back, axis=1, keepdims=True) * raw_cot).astype(BF)
    hidden_grad = against(out_grad, down_ref[0])
    gate, up = pre_act[:, :hidden_width], pre_act[:, hidden_width:]
    sig = jax.nn.sigmoid(gate)
    pre_grad = jnp.concatenate(
        [hidden_grad * up * sig * (1.0 + gate * (1.0 - sig)), hidden_grad * gate * sig], axis=1
    ).astype(BF)
    return raw_cot, out_grad, pre_grad


def own_forward(sources, cap, info, *refs):
    packed, refs = refs[:sources], refs[sources:]
    note_refs, refs = refs[:sources], refs[sources:]
    gate_ref, down_ref, refs = refs[0], refs[1], refs[2:]
    part_refs, refs = refs[:sources], refs[sources:]
    input_ref, pre_ref, hidden_ref, output_ref, tok, total = refs
    e = pl.program_id(0)
    count = tok.shape[0] // sources

    @pl.when(e == 0)
    def _():
        for s in range(sources):
            tok[s * count:(s + 1) * count, :] = packed[s][...]
        total[...] = jnp.zeros_like(total)

    picks, weights = routing_tile(note_refs, info[0] + e, count, cap)
    pick = selected(picks, [1.0] * sources).astype(BF)
    back = selected(picks, weights)
    inputs, pre_act, hidden = forward_tile(pick, tok, gate_ref, hidden_ref.shape[2])
    outputs = jnp.dot(hidden, down_ref[0], preferred_element_type=F32).astype(BF)
    input_ref[0] = inputs
    pre_ref[0] = pre_act
    hidden_ref[0] = hidden
    output_ref[0] = outputs
    total[...] += across(back.astype(BF), outputs)

    @pl.when(e == pl.num_programs(0) - 1)
    def _():
        for s in range(sources):
            part_refs[s][...] = total[s * count:(s + 1) * count, :].astype(BF)


def own_backward(sources, cap, info, *refs):
    cots, refs = refs[:sources], refs[sources:]
    note_refs, refs = refs[:sources], refs[sources:]
    gate_ref, down_ref, pre_ref, output_ref, refs = refs[0], refs[1], refs[2], refs[3], refs[4:]
    part_refs, refs = refs[:sources], refs[sources:]
    prob_ref, out_grad_ref, pre_grad_ref, cot, total = refs
    e = pl.program_id(0)
    count = cot.shape[0] // sources

    @pl.when(e == 0)
    def _():
        for s in range(sources):
            cot[s * count:(s + 1) * count, :] = cots[s][...]
        total[...] = jnp.zeros_like(total)

    picks, weights = routing_tile(note_refs, info[0] + e, count, cap)
    pick = selected(picks, [1.0] * sources).astype(BF)
    back = selected(picks, weights)
    hidden_width = pre_ref.shape[2] // 2
    raw_cot, out_grad, pre_grad = backward_tile(pick, back, cot, down_ref, pre_ref[0], hidden_width)
    out_grad_ref[0] = out_grad
    pre_grad_ref[0] = pre_grad
    slot_prob = jnp.sum(raw_cot * output_ref[0].astype(F32), axis=1, keepdims=True)
    for s in range(sources):
        prob_ref[s, pl.ds(e, 1), :] = jnp.sum(jnp.where(picks[s], slot_prob, 0.0), axis=0, keepdims=True)
    input_grad = against(pre_grad, gate_ref[0]).astype(BF)
    total[...] += across(pick, input_grad)

    @pl.when(e == pl.num_programs(0) - 1)
    def _():
        for s in range(sources):
            part_refs[s][...] = total[s * count:(s + 1) * count, :].astype(BF)


def far_gradients(sources, cap, info, *refs):
    packed, refs = refs[:sources], refs[sources:]
    note_refs, refs = refs[:sources], refs[sources:]
    cots, refs = refs[:sources], refs[sources:]
    gate_ref, down_ref, input_ref, hidden_ref, out_grad_ref, pre_grad_ref = refs[:6]
    gate_own, gate_share, down_own, down_share = refs[6:10]
    tok, cot, all_inputs, all_hidden, all_grads, all_pre, gate_sum, down_sum = refs[10:]
    e = pl.program_id(0)
    count = tok.shape[0] // sources
    slots = sources * cap

    @pl.when(e == 0)
    def _():
        for s in range(sources):
            tok[s * count:(s + 1) * count, :] = packed[s][...]
            cot[s * count:(s + 1) * count, :] = cots[s][...]

    picks, weights = routing_tile(note_refs, info[0] + e, count, cap)
    pick = selected(picks, [1.0] * sources).astype(BF)
    back = selected(picks, weights)
    hidden_width = hidden_ref.shape[2]
    inputs, pre_act, hidden = forward_tile(pick, tok, gate_ref, hidden_width)
    _, out_grad, pre_grad = backward_tile(pick, back, cot, down_ref, pre_act, hidden_width)
    for scratch, own, far in (
        (all_inputs, input_ref, inputs), (all_hidden, hidden_ref, hidden),
        (all_grads, out_grad_ref, out_grad), (all_pre, pre_grad_ref, pre_grad),
    ):
        scratch[:slots, :] = own[0]
        scratch[slots:, :] = far

    place, core = info[1], info[2]
    for left, right, total, own, share in (
        (all_hidden, all_grads, down_sum, down_own, down_share),
        (all_inputs, all_pre, gate_sum, gate_own, gate_share),
    ):
        size, block = total.shape[0], own.shape[1]
        columns = pl.ds(pl.multiple_of(place * size, size), size)
        total[...] = across(left[:, columns], right[...])
        own[0] = total[pl.ds(pl.multiple_of(core * block, block), block), :]
        share[0] = total[pl.ds(pl.multiple_of((1 - core) * block, block), block), :].astype(BF)


def joined(local, own_ref, share_ref, out_ref):
    for e in range(local):
        out_ref[:, e, :] = own_ref[e] + share_ref[e].astype(F32)


def whole(*shape):
    return pl.BlockSpec(shape, lambda e, info: (0,) * len(shape))


def each(*shape):
    return pl.BlockSpec((1,) + shape, lambda e, info: (e,) + (0,) * len(shape))


def kernel_call(body, grid, in_specs, out_specs, out_shape, scratch, flops, moved, grant):
    return pl.pallas_call(
        body,
        grid_spec=pltpu.PrefetchScalarGridSpec(
            num_scalar_prefetch=1, grid=(grid,), in_specs=in_specs, out_specs=out_specs, scratch_shapes=scratch
        ),
        out_shape=out_shape,
        compiler_params=pltpu.CompilerParams(vmem_limit_bytes=grant << 20),
        cost_estimate=pl.CostEstimate(flops=flops, bytes_accessed=moved, transcendentals=0),
    )


def two_chips(tokens, expert_ids, gate_probs, cotangent, gate_up, down_weights, *, sources, replicas):
    count, width = tokens.shape
    top = expert_ids.shape[1]
    local = gate_up.shape[1]
    hidden_width = down_weights.shape[0]
    pre_width = gate_up.shape[2]
    cap = min(CAP, count)
    along = replicas // CORES
    replica = lax.axis_index("replica")
    core, place = lax.rem(replica, CORES), lax.div(replica, CORES)
    home = lax.axis_index("expert")
    slots = sources * cap
    info = jnp.stack([home * local, place, core]).astype(jnp.int32)

    def to_source(values, shift):
        step = [(i, (i + shift) % sources) for i in range(sources)]
        return lax.ppermute(values, "expert", step) if shift else values

    def to_chip(values):
        step = [
            (x * CORES + c, ((x + 1) % along) * CORES + c)
            for x in range(along) for c in range(CORES)
        ]
        return lax.ppermute(values, "replica", step)

    fill = ((0, HALF - top), (0, 0))
    notes = jnp.concatenate(
        [jnp.pad(expert_ids.T.astype(BF), fill, constant_values=-1), jnp.pad(gate_probs.T, fill)], axis=1
    )
    packed = jnp.concatenate([tokens, jnp.pad(notes, ((0, 0), (0, width - 2 * count)))], axis=0)

    def gathered(values):
        far = [to_chip(values)]
        held = [to_source(values, s) for s in range(sources)]
        far += [to_chip(h) for h in held[1:]]
        return held, far

    near_packed, far_packed = gathered(packed)
    near_cots, far_cots = gathered(cotangent)
    gate_rows = lax.optimization_barrier(
        with_layout_constraint(gate_up.swapaxes(0, 1), Layout((0, 1, 2)))
    )
    down_rows = lax.optimization_barrier(
        with_layout_constraint(down_weights.swapaxes(0, 1), Layout((0, 1, 2)))
    )

    block_specs = [whole(count, width)] * sources
    note_specs = [pl.BlockSpec((HALF, 2 * count), lambda e, info: (count // HALF, 0))] * sources
    weight_specs = [each(width, pre_width), each(hidden_width, width)]
    block_shape = jax.ShapeDtypeStruct((count, width), BF)
    gathered_rows = pltpu.VMEM((sources * count, width), BF)
    part_total = pltpu.VMEM((sources * count, width), F32)

    def array(size, dtype, rows=slots):
        return jax.ShapeDtypeStruct((local, rows, size), dtype)

    product = 2 * local * slots * width * hidden_width
    weight_bytes = 6 * local * width * hidden_width
    *out_parts, inputs, pre_act, hidden, outputs = kernel_call(
        functools.partial(own_forward, sources, cap),
        local,
        block_specs + note_specs + weight_specs,
        block_specs + [each(slots, width), each(slots, pre_width), each(slots, hidden_width), each(slots, width)],
        [block_shape] * sources + [array(width, BF), array(pre_width, F32), array(hidden_width, BF), array(width, BF)],
        [gathered_rows, part_total],
        4 * product,
        2 * weight_bytes,
        FWD,
    )(info, *near_packed, *near_packed, gate_rows, down_rows)

    def returned(parts):
        return [to_source(parts[s], -s) for s in range(sources)]

    def added(arrived):
        return sum([a.astype(F32) for a in arrived[1:]], arrived[0].astype(F32)).astype(BF)

    out_arrived = returned(out_parts)

    *grad_parts, prob_part, out_grad, pre_grad = kernel_call(
        functools.partial(own_backward, sources, cap),
        local,
        block_specs + note_specs + weight_specs + [each(slots, pre_width), each(slots, width)],
        block_specs + [whole(sources, local, count), each(slots, width), each(slots, pre_width)],
        [block_shape] * sources + [
            jax.ShapeDtypeStruct((sources, local, count), F32), array(width, BF), array(pre_width, BF)
        ],
        [gathered_rows, part_total],
        4 * product,
        2 * weight_bytes,
        BWD,
    )(info, *near_cots, *near_packed, gate_rows, down_rows, pre_act, outputs)
    prob_arrived = [to_source(prob_part[s], -s) for s in range(sources)]
    grad_arrived = returned(grad_parts)

    gate_block, down_block = width // replicas, hidden_width // replicas
    gate_own, gate_share, down_own, down_share = kernel_call(
        functools.partial(far_gradients, sources, cap),
        local,
        block_specs + note_specs + block_specs + weight_specs + [
            each(slots, width), each(slots, hidden_width), each(slots, width), each(slots, pre_width)
        ],
        [
            each(gate_block, pre_width), each(gate_block, pre_width),
            each(down_block, width), each(down_block, width),
        ],
        [
            array(pre_width, F32, gate_block), array(pre_width, BF, gate_block),
            array(width, F32, down_block), array(width, BF, down_block),
        ],
        [
            gathered_rows, gathered_rows,
            pltpu.VMEM((2 * slots, width), BF), pltpu.VMEM((2 * slots, hidden_width), BF),
            pltpu.VMEM((2 * slots, width), BF), pltpu.VMEM((2 * slots, pre_width), BF),
            pltpu.VMEM((CORES * gate_block, pre_width), F32), pltpu.VMEM((CORES * down_block, width), F32),
        ],
        6 * product,
        3 * weight_bytes,
        FAR,
    )(
        info, *far_packed, *far_packed, *far_cots, gate_rows, down_rows,
        inputs, hidden, out_grad, pre_grad,
    )

    pair = [(i, i ^ 1) for i in range(replicas)]

    def final(own, share):
        theirs = lax.ppermute(share, "replica", pair)
        rows, size = own.shape[1], own.shape[2]
        cut = rows // 4
        return pl.pallas_call(
            functools.partial(joined, local),
            grid=(rows // cut,),
            in_specs=[pl.BlockSpec((local, cut, size), lambda i: (0, i, 0))] * 2,
            out_specs=pl.BlockSpec((cut, local, size), lambda i: (i, 0, 0)),
            out_shape=jax.ShapeDtypeStruct((rows, local, size), F32),
            compiler_params=pltpu.CompilerParams(vmem_limit_bytes=JOIN << 20),
            cost_estimate=pl.CostEstimate(flops=0, bytes_accessed=10 * own.size, transcendentals=0),
        )(own, theirs)

    gate_up_gradient = final(gate_own, gate_share)
    down_gradient = final(down_own, down_share)

    choice = expert_ids.T
    prob_gradient = jnp.zeros((top, count), F32)
    for s in range(sources):
        block = lax.rem(home + s, sources) * local
        hit = choice[:, None, :] == (block + jnp.arange(local, dtype=jnp.int32))[None, :, None]
        prob_gradient = prob_gradient + jnp.sum(jnp.where(hit, prob_arrived[s][None], 0.0), axis=1)
    return (added(out_arrived), added(grad_arrived), prob_gradient.T, gate_up_gradient, down_gradient)


def on_device(*args, sources, replicas):
    count, top, local = args[0].shape[0], args[1].shape[1], args[4].shape[1]
    small = sources * min(CAP, count) * local <= 1024 and sources <= 4
    plain = replicas == 2 * CORES and small and count % 128 == 0 and top <= HALF and 2 * count <= args[0].shape[1]
    return (two_chips if plain else general)(*args, sources=sources, replicas=replicas)


def solution(mesh):
    rows = P(("groups", "expert", "replica"), None)
    sources, replicas = mesh.shape["expert"], mesh.shape["replica"]

    def body(*args):
        return on_device(*args, sources=sources, replicas=replicas)

    return jax.shard_map(
        body,
        mesh=mesh,
        in_specs=(rows, rows, rows, rows, P(None, "expert", None), P(None, "expert", None)),
        out_specs=(
            rows,
            rows,
            rows,
            P(("groups", "replica"), "expert", None),
            P(("groups", "replica"), "expert", None),
        ),
        check_vma=False,
    )
```

```python
import functools

import jax
import jax.numpy as jnp
from jax import lax
from jax.experimental import pallas as pl
from jax.experimental.pallas import tpu as pltpu
from jax.experimental.layout import Layout, with_layout_constraint
from jax.sharding import PartitionSpec as P


CAP = 64
CORES = 2
BF = jnp.bfloat16
F32 = jnp.float32


def general(tokens, expert_ids, gate_probs, cotangent, gate_up, down_weights, *, sources, replicas):
    count, width = tokens.shape
    top = expert_ids.shape[1]
    local = gate_up.shape[1]
    hidden_width = down_weights.shape[0]
    cap = min(CAP, count)
    along = replicas // CORES
    replica = lax.axis_index("replica")
    core, place = lax.rem(replica, CORES), lax.div(replica, CORES)
    first = lax.axis_index("expert") * local
    slots = sources * cap

    def to_source(values, shift):
        step = [(i, (i + shift) % sources) for i in range(sources)]
        return lax.ppermute(values, "expert", step) if shift else values

    def to_chip(values, shift):
        step = [
            (x * CORES + c, ((x + shift) % along) * CORES + c)
            for x in range(along) for c in range(CORES)
        ]
        return lax.ppermute(values, "replica", step)

    notes = jnp.concatenate([expert_ids.T.astype(BF), gate_probs.T], axis=0)
    flat = notes.reshape(-1)
    extra = -(-flat.shape[0] // (16 * width)) * 16
    flat = jnp.pad(flat, (0, extra * width - flat.shape[0])).reshape(extra, width)
    packed = jnp.concatenate([tokens, flat], axis=0)

    def gathered(values):
        others = [[to_chip(values, t)] for t in range(1, along)]
        held = [to_source(values, s) for s in range(sources)]
        if sources <= 4:
            pieces = [[h] for h in held[1:]]
        else:
            pieces = [held[1:]]
        for piece in pieces:
            sent = piece[0] if len(piece) == 1 else jnp.stack(piece)
            for t in range(1, along):
                got = to_chip(sent, t)
                others[t - 1] += [got] if len(piece) == 1 else [got[i] for i in range(len(piece))]
        return [held] + others

    all_packed = gathered(packed)
    all_cots = gathered(cotangent)

    gate_rows = lax.optimization_barrier(
        with_layout_constraint(gate_up.swapaxes(0, 1), Layout((0, 1, 2)))
    )
    down_rows = lax.optimization_barrier(
        with_layout_constraint(down_weights.swapaxes(0, 1), Layout((0, 1, 2)))
    )

    ahead = (jnp.arange(count)[:, None] < jnp.arange(count)[None, :]).astype(BF)
    same = jnp.arange(sources)[:, None] == jnp.arange(sources)[None, :]

    def routing(held):
        all_notes = jnp.stack([h[count:].reshape(-1)[:notes.size].reshape(notes.shape) for h in held])
        all_ids = all_notes[:, :top].astype(jnp.int32)
        all_probs = all_notes[:, top:]
        named = (all_ids[None] == (first + jnp.arange(local, dtype=jnp.int32))[:, None, None, None])
        member = jnp.any(named, axis=2)
        weight = jnp.sum(jnp.where(named, all_probs[None].astype(F32), 0.0), axis=2)
        rank = jnp.einsum("esp,pq->esq", member.astype(BF), ahead, preferred_element_type=F32)
        rank = jnp.where(member, rank.astype(jnp.int32), -1)
        chosen = rank[:, :, None, :] == jnp.arange(cap, dtype=jnp.int32)[None, None, :, None]
        wide = chosen[:, :, :, None, :] & same[None, :, None, :, None]
        pick = wide.astype(BF).reshape(local * slots, sources * count)
        slot_weight = jnp.sum(jnp.where(chosen, weight[:, :, None, :], 0.0), axis=3).reshape(local, slots, 1)
        return weight, chosen, wide, pick, slot_weight

    def rows(pick, values):
        return jnp.dot(pick, values, preferred_element_type=F32).astype(BF).reshape(local, slots, width)

    def forward(held):
        weight, chosen, wide, pick, slot_weight = routing(held)
        inputs = rows(pick, jnp.concatenate([h[:count] for h in held], axis=0))
        pre_act = jnp.einsum("erd,edf->erf", inputs, gate_rows, preferred_element_type=F32)
        gate, up = pre_act[..., :hidden_width], pre_act[..., hidden_width:]
        sig = jax.nn.sigmoid(gate)
        hidden = (gate * sig * up).astype(BF)
        return (weight, chosen, wide, pick, slot_weight), inputs, gate, up, sig, hidden

    def backward(route, held, gate, up, sig):
        _, _, _, pick, slot_weight = route
        raw_cot = rows(pick, jnp.concatenate(held, axis=0))
        out_grad = (slot_weight * raw_cot.astype(F32)).astype(BF)
        hidden_grad = jnp.einsum("erd,efd->erf", out_grad, down_rows, preferred_element_type=F32)
        pre_grad = jnp.concatenate(
            [hidden_grad * up * sig * (1.0 + gate * (1.0 - sig)), hidden_grad * gate * sig], axis=-1
        ).astype(BF)
        return raw_cot, out_grad, pre_grad

    def returned(matrix, values):
        parts = jnp.einsum(
            "ra,rd->ad", matrix, values.reshape(local * slots, width), preferred_element_type=F32
        ).astype(BF).reshape(sources, count, width)
        arrived = [to_source(parts[s], -s).astype(F32) for s in range(sources)]
        return sum(arrived[1:], arrived[0]).astype(BF)

    route, inputs, gate, up, sig, hidden = forward(all_packed[0])
    weight, chosen, wide, pick, _ = route
    outputs = jnp.einsum("erf,efd->erd", hidden, down_rows, preferred_element_type=F32).astype(BF)
    back = jnp.where(wide, weight[:, :, None, None, :], 0.0).astype(BF).reshape(local * slots, sources * count)
    combined = returned(back, outputs)
    raw_cot, out_grad, pre_grad = backward(route, all_cots[0], gate, up, sig)
    input_grad = jnp.einsum("erf,edf->erd", pre_grad, gate_rows, preferred_element_type=F32).astype(BF)
    token_gradient = returned(pick, input_grad)

    all_inputs, all_hidden, all_grads, all_pre = [inputs], [hidden], [out_grad], [pre_grad]
    for t in range(1, along):
        route_t, inputs_t, gate_t, up_t, sig_t, hidden_t = forward(all_packed[t])
        _, out_grad_t, pre_grad_t = backward(route_t, all_cots[t], gate_t, up_t, sig_t)
        all_inputs.append(inputs_t)
        all_hidden.append(hidden_t)
        all_grads.append(out_grad_t)
        all_pre.append(pre_grad_t)

    pair = [(i, i ^ 1) for i in range(replicas)]

    def columns(values, side):
        size = values.shape[-1] // replicas
        return lax.dynamic_slice_in_dim(values, (place * CORES + side) * size, size, 2)

    def gradient(left, right):
        right = jnp.concatenate(right, axis=1)

        def part(side):
            chosen_columns = jnp.concatenate([columns(l, side) for l in left], axis=1)
            return jnp.einsum("era,erb->eab", chosen_columns, right, preferred_element_type=F32)

        share = with_layout_constraint(part(1 - core).astype(BF).swapaxes(0, 1), Layout((0, 1, 2)))
        theirs = lax.ppermute(share, "replica", pair)
        own = with_layout_constraint(part(core).swapaxes(0, 1), Layout((0, 1, 2)))
        return own + theirs.astype(F32)

    down_gradient = gradient(all_hidden, all_grads)
    gate_up_gradient = gradient(all_inputs, all_pre)

    slot_prob = jnp.sum(raw_cot.astype(F32) * outputs.astype(F32), axis=2).reshape(local, sources, cap, 1)
    prob_part = jnp.sum(jnp.where(chosen, slot_prob, 0.0), axis=2).swapaxes(0, 1)
    choice = expert_ids.T
    prob_gradient = jnp.zeros((top, count), F32)
    home = lax.axis_index("expert")
    for s in range(sources):
        block = lax.rem(home + s, sources) * local
        theirs = to_source(prob_part[s], -s)
        hit = choice[:, None, :] == (block + jnp.arange(local, dtype=jnp.int32))[None, :, None]
        prob_gradient = prob_gradient + jnp.sum(jnp.where(hit, theirs[None], 0.0), axis=1)
    prob_gradient = prob_gradient.T
    return (combined, token_gradient, prob_gradient, gate_up_gradient, down_gradient)


HALF = 8
FWD, BWD, FAR, JOIN = 24, 24, 28, 8


def routing_tile(note_refs, expert, count, cap):
    members, weights = [], []
    for ref in note_refs:
        tile = ref[...].astype(F32)
        named = tile[:, :count].astype(jnp.int32) == expert
        members.append(jnp.max(jnp.where(named, 1.0, 0.0), axis=0, keepdims=True))
        weights.append(jnp.sum(jnp.where(named, tile[:, count:], 0.0), axis=0, keepdims=True))
    member = jnp.concatenate(members, axis=0)
    ahead = (
        lax.broadcasted_iota(jnp.int32, (count, count), 0) < lax.broadcasted_iota(jnp.int32, (count, count), 1)
    )
    ahead = jnp.where(ahead, 1.0, 0.0).astype(BF)
    rank = jnp.dot(member.astype(BF), ahead, preferred_element_type=F32).astype(jnp.int32)
    slots = len(note_refs) * cap
    row = lax.broadcasted_iota(jnp.int32, (slots, count), 0)
    picks = []
    for s in range(len(note_refs)):
        place = jnp.where(members[s] > 0.0, rank[s:s + 1] + s * cap, -1)
        picks.append(row == place)
    return picks, weights


def selected(picks, values):
    return jnp.concatenate([jnp.where(p, v, 0.0) for p, v in zip(picks, values)], axis=1)


def across(left, right):
    return lax.dot_general(left, right, (((0,), (0,)), ((), ())), preferred_element_type=F32)


def against(left, right):
    return lax.dot_general(left, right, (((1,), (1,)), ((), ())), preferred_element_type=F32)


def forward_tile(pick, tok, gate_ref, hidden_width):
    inputs = jnp.dot(pick, tok[...], preferred_element_type=F32).astype(BF)
    pre_act = jnp.dot(inputs, gate_ref[0], preferred_element_type=F32)
    gate, up = pre_act[:, :hidden_width], pre_act[:, hidden_width:]
    sig = jax.nn.sigmoid(gate)
    return inputs, pre_act, (gate * sig * up).astype(BF)


def backward_tile(pick, back, cot, down_ref, pre_act, hidden_width):
    raw_cot = jnp.dot(pick, cot[...], preferred_element_type=F32)
    out_grad = (jnp.sum(back, axis=1, keepdims=True) * raw_cot).astype(BF)
    hidden_grad = against(out_grad, down_ref[0])
    gate, up = pre_act[:, :hidden_width], pre_act[:, hidden_width:]
    sig = jax.nn.sigmoid(gate)
    pre_grad = jnp.concatenate(
        [hidden_grad * up * sig * (1.0 + gate * (1.0 - sig)), hidden_grad * gate * sig], axis=1
    ).astype(BF)
    return raw_cot, out_grad, pre_grad


def own_forward(sources, cap, info, *refs):
    packed, refs = refs[:sources], refs[sources:]
    note_refs, refs = refs[:sources], refs[sources:]
    gate_ref, down_ref, refs = refs[0], refs[1], refs[2:]
    part_refs, refs = refs[:sources], refs[sources:]
    input_ref, pre_ref, hidden_ref, output_ref, tok, total = refs
    e = pl.program_id(0)
    count = tok.shape[0] // sources

    @pl.when(e == 0)
    def _():
        for s in range(sources):
            tok[s * count:(s + 1) * count, :] = packed[s][...]
        total[...] = jnp.zeros_like(total)

    picks, weights = routing_tile(note_refs, info[0] + e, count, cap)
    pick = selected(picks, [1.0] * sources).astype(BF)
    back = selected(picks, weights)
    inputs, pre_act, hidden = forward_tile(pick, tok, gate_ref, hidden_ref.shape[2])
    outputs = jnp.dot(hidden, down_ref[0], preferred_element_type=F32).astype(BF)
    input_ref[0] = inputs
    pre_ref[0] = pre_act
    hidden_ref[0] = hidden
    output_ref[0] = outputs
    total[...] += across(back.astype(BF), outputs)

    @pl.when(e == pl.num_programs(0) - 1)
    def _():
        for s in range(sources):
            part_refs[s][...] = total[s * count:(s + 1) * count, :].astype(BF)


def own_backward(sources, cap, info, *refs):
    cots, refs = refs[:sources], refs[sources:]
    note_refs, refs = refs[:sources], refs[sources:]
    gate_ref, down_ref, pre_ref, output_ref, refs = refs[0], refs[1], refs[2], refs[3], refs[4:]
    part_refs, refs = refs[:sources], refs[sources:]
    prob_ref, out_grad_ref, pre_grad_ref, cot, total = refs
    e = pl.program_id(0)
    count = cot.shape[0] // sources

    @pl.when(e == 0)
    def _():
        for s in range(sources):
            cot[s * count:(s + 1) * count, :] = cots[s][...]
        total[...] = jnp.zeros_like(total)

    picks, weights = routing_tile(note_refs, info[0] + e, count, cap)
    pick = selected(picks, [1.0] * sources).astype(BF)
    back = selected(picks, weights)
    hidden_width = pre_ref.shape[2] // 2
    raw_cot, out_grad, pre_grad = backward_tile(pick, back, cot, down_ref, pre_ref[0], hidden_width)
    out_grad_ref[0] = out_grad
    pre_grad_ref[0] = pre_grad
    slot_prob = jnp.sum(raw_cot * output_ref[0].astype(F32), axis=1, keepdims=True)
    for s in range(sources):
        prob_ref[s, pl.ds(e, 1), :] = jnp.sum(jnp.where(picks[s], slot_prob, 0.0), axis=0, keepdims=True)
    input_grad = against(pre_grad, gate_ref[0]).astype(BF)
    total[...] += across(pick, input_grad)

    @pl.when(e == pl.num_programs(0) - 1)
    def _():
        for s in range(sources):
            part_refs[s][...] = total[s * count:(s + 1) * count, :].astype(BF)


def far_gradients(sources, cap, info, *refs):
    packed, refs = refs[:sources], refs[sources:]
    note_refs, refs = refs[:sources], refs[sources:]
    cots, refs = refs[:sources], refs[sources:]
    gate_ref, down_ref, input_ref, hidden_ref, out_grad_ref, pre_grad_ref = refs[:6]
    gate_own, gate_share, down_own, down_share = refs[6:10]
    tok, cot, all_inputs, all_hidden, all_grads, all_pre, down_sum = refs[10:]
    e = pl.program_id(0)
    count = tok.shape[0] // sources
    slots = sources * cap

    @pl.when(e == 0)
    def _():
        for s in range(sources):
            tok[s * count:(s + 1) * count, :] = packed[s][...]
            cot[s * count:(s + 1) * count, :] = cots[s][...]

    picks, weights = routing_tile(note_refs, info[0] + e, count, cap)
    pick = selected(picks, [1.0] * sources).astype(BF)
    back = selected(picks, weights)
    hidden_width = hidden_ref.shape[2]
    inputs, pre_act, hidden = forward_tile(pick, tok, gate_ref, hidden_width)
    _, out_grad, pre_grad = backward_tile(pick, back, cot, down_ref, pre_act, hidden_width)
    for scratch, own, far in (
        (all_inputs, input_ref, inputs), (all_hidden, hidden_ref, hidden),
        (all_grads, out_grad_ref, out_grad), (all_pre, pre_grad_ref, pre_grad),
    ):
        scratch[:slots, :] = own[0]
        scratch[slots:, :] = far

    place, core = info[1], info[2]

    def block(index, size):
        return pl.ds(pl.multiple_of(index * size, size), size)

    size = gate_own.shape[1]
    gate_own[0] = across(all_inputs[:, block(place * CORES + core, size)], all_pre[...])
    gate_share[0] = across(all_inputs[:, block(place * CORES + 1 - core, size)], all_pre[...]).astype(BF)
    size = down_own.shape[1]
    down_sum[...] = across(all_hidden[:, block(place, CORES * size)], all_grads[...])
    down_own[0] = down_sum[block(core, size), :]
    down_share[0] = down_sum[block(1 - core, size), :].astype(BF)


def joined(local, gate_own, gate_share, down_own, down_share, gate_out, down_out):
    for own, share, out in ((gate_own, gate_share, gate_out), (down_own, down_share, down_out)):
        for e in range(local):
            out[:, e, :] = own[e] + share[e].astype(F32)


def summed(sources, *refs):
    for first, out in ((0, refs[-2]), (sources, refs[-1])):
        total = refs[first][...].astype(F32)
        for ref in refs[first + 1:first + sources]:
            total += ref[...].astype(F32)
        out[...] = total.astype(BF)


def whole(*shape):
    return pl.BlockSpec(shape, lambda e, info: (0,) * len(shape))


def each(*shape):
    return pl.BlockSpec((1,) + shape, lambda e, info: (e,) + (0,) * len(shape))


def kernel_call(body, grid, in_specs, out_specs, out_shape, scratch, flops, moved, grant):
    return pl.pallas_call(
        body,
        grid_spec=pltpu.PrefetchScalarGridSpec(
            num_scalar_prefetch=1, grid=(grid,), in_specs=in_specs, out_specs=out_specs, scratch_shapes=scratch
        ),
        out_shape=out_shape,
        compiler_params=pltpu.CompilerParams(vmem_limit_bytes=grant << 20),
        cost_estimate=pl.CostEstimate(flops=flops, bytes_accessed=moved, transcendentals=0),
    )


def two_chips(tokens, expert_ids, gate_probs, cotangent, gate_up, down_weights, *, sources, replicas):
    count, width = tokens.shape
    top = expert_ids.shape[1]
    local = gate_up.shape[1]
    hidden_width = down_weights.shape[0]
    pre_width = gate_up.shape[2]
    cap = min(CAP, count)
    along = replicas // CORES
    replica = lax.axis_index("replica")
    core, place = lax.rem(replica, CORES), lax.div(replica, CORES)
    home = lax.axis_index("expert")
    slots = sources * cap
    info = jnp.stack([home * local, place, core]).astype(jnp.int32)

    def to_mate(values, mask):
        return lax.ppermute(values, "expert", [(i, i ^ mask) for i in range(sources)]) if mask else values

    def to_chip(values):
        step = [
            (x * CORES + c, ((x + 1) % along) * CORES + c)
            for x in range(along) for c in range(CORES)
        ]
        return lax.ppermute(values, "replica", step)

    fill = ((0, HALF - top), (0, 0))
    notes = jnp.concatenate(
        [jnp.pad(expert_ids.T.astype(BF), fill, constant_values=-1), jnp.pad(gate_probs.T, fill)], axis=1
    )
    packed = jnp.concatenate([tokens, jnp.pad(notes, ((0, 0), (0, width - 2 * count)))], axis=0)

    far_own = to_chip(jnp.concatenate([packed, cotangent], axis=0))

    def gathered(values):
        held = [values] * sources
        for mask in range(1, sources):
            low = mask & -mask
            held[mask] = to_mate(held[mask - low], low)
        far = [to_chip(h) for h in held[1:]]
        return held, far

    near_packed, far_packed = gathered(packed)
    near_cots, far_cots = gathered(cotangent)
    far_packed = [far_own[:packed.shape[0]]] + far_packed
    far_cots = [far_own[packed.shape[0]:]] + far_cots

    always = lax.optimization_barrier(jnp.ones((), jnp.bool_))

    def in_hbm(values):
        return pltpu.with_memory_space_constraint(values, pltpu.HBM)

    def by_expert(weights):
        moved = with_layout_constraint(weights.swapaxes(0, 1), Layout((0, 1, 2)))
        return in_hbm(lax.optimization_barrier(moved))

    down_rows = by_expert(down_weights)
    gate_rows = by_expert(jnp.where(always, gate_up, jnp.zeros((), BF)))

    block_specs = [whole(count, width)] * sources
    note_specs = [pl.BlockSpec((HALF, 2 * count), lambda e, info: (count // HALF, 0))] * sources
    weight_specs = [each(width, pre_width), each(hidden_width, width)]
    block_shape = jax.ShapeDtypeStruct((count, width), BF)
    gathered_rows = pltpu.VMEM((sources * count, width), BF)
    part_total = pltpu.VMEM((sources * count, width), F32)

    def array(size, dtype, rows=slots):
        return jax.ShapeDtypeStruct((local, rows, size), dtype)

    product = 2 * local * slots * width * hidden_width
    weight_bytes = 6 * local * width * hidden_width
    *out_parts, inputs, pre_act, hidden, outputs = kernel_call(
        functools.partial(own_forward, sources, cap),
        local,
        block_specs + note_specs + weight_specs,
        block_specs + [each(slots, width), each(slots, pre_width), each(slots, hidden_width), each(slots, width)],
        [block_shape] * sources + [array(width, BF), array(pre_width, F32), array(hidden_width, BF), array(width, BF)],
        [gathered_rows, part_total],
        4 * product,
        2 * weight_bytes,
        FWD,
    )(info, *near_packed, *near_packed, gate_rows, down_rows)

    def returned(parts):
        return [to_mate(parts[s], s) for s in range(sources)]

    out_arrived = returned(out_parts)

    *grad_parts, prob_part, out_grad, pre_grad = kernel_call(
        functools.partial(own_backward, sources, cap),
        local,
        block_specs + note_specs + weight_specs + [each(slots, pre_width), each(slots, width)],
        block_specs + [whole(sources, local, count), each(slots, width), each(slots, pre_width)],
        [block_shape] * sources + [
            jax.ShapeDtypeStruct((sources, local, count), F32), array(width, BF), array(pre_width, BF)
        ],
        [gathered_rows, part_total],
        4 * product,
        2 * weight_bytes,
        BWD,
    )(info, *near_cots, *near_packed, gate_rows, down_rows, pre_act, outputs)
    prob_arrived = [to_mate(prob_part[s], s) for s in range(sources)]
    grad_arrived = returned(grad_parts)

    gate_block, down_block = width // replicas, hidden_width // replicas
    gate_own, gate_share, down_own, down_share = kernel_call(
        functools.partial(far_gradients, sources, cap),
        local,
        block_specs + note_specs + block_specs + weight_specs + [
            each(slots, width), each(slots, hidden_width), each(slots, width), each(slots, pre_width)
        ],
        [
            each(gate_block, pre_width), each(gate_block, pre_width),
            each(down_block, width), each(down_block, width),
        ],
        [
            pltpu.HBM((local, gate_block, pre_width), F32), array(pre_width, BF, gate_block),
            pltpu.HBM((local, down_block, width), F32), array(width, BF, down_block),
        ],
        [
            gathered_rows, gathered_rows,
            pltpu.VMEM((2 * slots, width), BF), pltpu.VMEM((2 * slots, hidden_width), BF),
            pltpu.VMEM((2 * slots, width), BF), pltpu.VMEM((2 * slots, pre_width), BF),
            pltpu.VMEM((CORES * down_block, width), F32),
        ],
        6 * product,
        3 * weight_bytes,
        FAR,
    )(
        info, *far_packed, *far_packed, *far_cots, gate_rows, down_rows,
        inputs, hidden, out_grad, pre_grad,
    )

    pair = [(i, i ^ 1) for i in range(replicas)]
    down_theirs, gate_theirs = lax.ppermute(down_share, "replica", pair), lax.ppermute(gate_share, "replica", pair)

    combined, token_gradient = pl.pallas_call(
        functools.partial(summed, sources),
        name="summed",
        grid=(2,),
        in_specs=[pl.BlockSpec((count // 2, width), lambda i: (i, 0))] * (2 * sources),
        out_specs=[pl.BlockSpec((count // 2, width), lambda i: (i, 0))] * 2,
        out_shape=[block_shape] * 2,
        compiler_params=pltpu.CompilerParams(vmem_limit_bytes=JOIN << 20),
        cost_estimate=pl.CostEstimate(flops=0, bytes_accessed=20 * count * width, transcendentals=0),
    )(*out_arrived, *grad_arrived)

    cuts = 8
    gate_cut, down_cut = gate_block // cuts, down_block // cuts

    def near_spec(cut, size):
        return pl.BlockSpec((local, cut, size), lambda i: (0, i, 0))

    def out_spec(cut, size):
        return pl.BlockSpec((cut, local, size), lambda i: (i, 0, 0))

    gate_up_gradient, down_gradient = pl.pallas_call(
        functools.partial(joined, local),
        name="joined",
        grid=(cuts,),
        in_specs=[near_spec(gate_cut, pre_width)] * 2 + [near_spec(down_cut, width)] * 2,
        out_specs=[out_spec(gate_cut, pre_width), out_spec(down_cut, width)],
        out_shape=[
            jax.ShapeDtypeStruct((gate_block, local, pre_width), F32),
            jax.ShapeDtypeStruct((down_block, local, width), F32),
        ],
        compiler_params=pltpu.CompilerParams(vmem_limit_bytes=JOIN << 20),
        cost_estimate=pl.CostEstimate(flops=0, bytes_accessed=10 * gate_own.size, transcendentals=0),
    )(in_hbm(gate_own), gate_theirs, in_hbm(down_own), down_theirs)

    choice = expert_ids.T
    prob_gradient = jnp.zeros((top, count), F32)
    for s in range(sources):
        block = jnp.bitwise_xor(home, s) * local
        hit = choice[:, None, :] == (block + jnp.arange(local, dtype=jnp.int32))[None, :, None]
        prob_gradient = prob_gradient + jnp.sum(jnp.where(hit, prob_arrived[s][None], 0.0), axis=1)
    return (combined, token_gradient, prob_gradient.T, gate_up_gradient, down_gradient)


def on_device(*args, sources, replicas):
    count, top, local = args[0].shape[0], args[1].shape[1], args[4].shape[1]
    small = sources * min(CAP, count) * local <= 1024 and sources <= 4
    plain = replicas == 2 * CORES and small and sources & (sources - 1) == 0 and args[0].shape[1] % (128 * replicas) == 0 and count % 128 == 0 and top <= HALF and 2 * count <= args[0].shape[1]
    return (two_chips if plain else general)(*args, sources=sources, replicas=replicas)


def solution(mesh):
    rows = P(("groups", "expert", "replica"), None)
    sources, replicas = mesh.shape["expert"], mesh.shape["replica"]

    def body(*args):
        return on_device(*args, sources=sources, replicas=replicas)

    return jax.shard_map(
        body,
        mesh=mesh,
        in_specs=(rows, rows, rows, rows, P(None, "expert", None), P(None, "expert", None)),
        out_specs=(
            rows,
            rows,
            rows,
            P(("groups", "replica"), "expert", None),
            P(("groups", "replica"), "expert", None),
        ),
        check_vma=False,
    )
```

```python
import functools

import jax
import jax.numpy as jnp
from jax import lax
from jax.experimental import pallas as pl
from jax.experimental.pallas import tpu as pltpu
from jax.experimental.layout import Layout, with_layout_constraint
from jax.sharding import PartitionSpec as P


CAP = 64
CORES = 2
BF = jnp.bfloat16
F32 = jnp.float32


def general(tokens, expert_ids, gate_probs, cotangent, gate_up, down_weights, *, sources, replicas):
    count, width = tokens.shape
    top = expert_ids.shape[1]
    local = gate_up.shape[1]
    hidden_width = down_weights.shape[0]
    cap = min(CAP, count)
    along = replicas // CORES
    replica = lax.axis_index("replica")
    core, place = lax.rem(replica, CORES), lax.div(replica, CORES)
    first = lax.axis_index("expert") * local
    slots = sources * cap

    def to_source(values, shift):
        step = [(i, (i + shift) % sources) for i in range(sources)]
        return lax.ppermute(values, "expert", step) if shift else values

    def to_chip(values, shift):
        step = [
            (x * CORES + c, ((x + shift) % along) * CORES + c)
            for x in range(along) for c in range(CORES)
        ]
        return lax.ppermute(values, "replica", step)

    notes = jnp.concatenate([expert_ids.T.astype(BF), gate_probs.T], axis=0)
    flat = notes.reshape(-1)
    extra = -(-flat.shape[0] // (16 * width)) * 16
    flat = jnp.pad(flat, (0, extra * width - flat.shape[0])).reshape(extra, width)
    packed = jnp.concatenate([tokens, flat], axis=0)

    def gathered(values):
        others = [[to_chip(values, t)] for t in range(1, along)]
        held = [to_source(values, s) for s in range(sources)]
        if sources <= 4:
            pieces = [[h] for h in held[1:]]
        else:
            pieces = [held[1:]]
        for piece in pieces:
            sent = piece[0] if len(piece) == 1 else jnp.stack(piece)
            for t in range(1, along):
                got = to_chip(sent, t)
                others[t - 1] += [got] if len(piece) == 1 else [got[i] for i in range(len(piece))]
        return [held] + others

    all_packed = gathered(packed)
    all_cots = gathered(cotangent)

    gate_rows = lax.optimization_barrier(
        with_layout_constraint(gate_up.swapaxes(0, 1), Layout((0, 1, 2)))
    )
    down_rows = lax.optimization_barrier(
        with_layout_constraint(down_weights.swapaxes(0, 1), Layout((0, 1, 2)))
    )

    ahead = (jnp.arange(count)[:, None] < jnp.arange(count)[None, :]).astype(BF)
    same = jnp.arange(sources)[:, None] == jnp.arange(sources)[None, :]

    def routing(held):
        all_notes = jnp.stack([h[count:].reshape(-1)[:notes.size].reshape(notes.shape) for h in held])
        all_ids = all_notes[:, :top].astype(jnp.int32)
        all_probs = all_notes[:, top:]
        named = (all_ids[None] == (first + jnp.arange(local, dtype=jnp.int32))[:, None, None, None])
        member = jnp.any(named, axis=2)
        weight = jnp.sum(jnp.where(named, all_probs[None].astype(F32), 0.0), axis=2)
        rank = jnp.einsum("esp,pq->esq", member.astype(BF), ahead, preferred_element_type=F32)
        rank = jnp.where(member, rank.astype(jnp.int32), -1)
        chosen = rank[:, :, None, :] == jnp.arange(cap, dtype=jnp.int32)[None, None, :, None]
        wide = chosen[:, :, :, None, :] & same[None, :, None, :, None]
        pick = wide.astype(BF).reshape(local * slots, sources * count)
        slot_weight = jnp.sum(jnp.where(chosen, weight[:, :, None, :], 0.0), axis=3).reshape(local, slots, 1)
        return weight, chosen, wide, pick, slot_weight

    def rows(pick, values):
        return jnp.dot(pick, values, preferred_element_type=F32).astype(BF).reshape(local, slots, width)

    def forward(held):
        weight, chosen, wide, pick, slot_weight = routing(held)
        inputs = rows(pick, jnp.concatenate([h[:count] for h in held], axis=0))
        pre_act = jnp.einsum("erd,edf->erf", inputs, gate_rows, preferred_element_type=F32)
        gate, up = pre_act[..., :hidden_width], pre_act[..., hidden_width:]
        sig = jax.nn.sigmoid(gate)
        hidden = (gate * sig * up).astype(BF)
        return (weight, chosen, wide, pick, slot_weight), inputs, gate, up, sig, hidden

    def backward(route, held, gate, up, sig):
        _, _, _, pick, slot_weight = route
        raw_cot = rows(pick, jnp.concatenate(held, axis=0))
        out_grad = (slot_weight * raw_cot.astype(F32)).astype(BF)
        hidden_grad = jnp.einsum("erd,efd->erf", out_grad, down_rows, preferred_element_type=F32)
        pre_grad = jnp.concatenate(
            [hidden_grad * up * sig * (1.0 + gate * (1.0 - sig)), hidden_grad * gate * sig], axis=-1
        ).astype(BF)
        return raw_cot, out_grad, pre_grad

    def returned(matrix, values):
        parts = jnp.einsum(
            "ra,rd->ad", matrix, values.reshape(local * slots, width), preferred_element_type=F32
        ).astype(BF).reshape(sources, count, width)
        arrived = [to_source(parts[s], -s).astype(F32) for s in range(sources)]
        return sum(arrived[1:], arrived[0]).astype(BF)

    route, inputs, gate, up, sig, hidden = forward(all_packed[0])
    weight, chosen, wide, pick, _ = route
    outputs = jnp.einsum("erf,efd->erd", hidden, down_rows, preferred_element_type=F32).astype(BF)
    back = jnp.where(wide, weight[:, :, None, None, :], 0.0).astype(BF).reshape(local * slots, sources * count)
    combined = returned(back, outputs)
    raw_cot, out_grad, pre_grad = backward(route, all_cots[0], gate, up, sig)
    input_grad = jnp.einsum("erf,edf->erd", pre_grad, gate_rows, preferred_element_type=F32).astype(BF)
    token_gradient = returned(pick, input_grad)

    all_inputs, all_hidden, all_grads, all_pre = [inputs], [hidden], [out_grad], [pre_grad]
    for t in range(1, along):
        route_t, inputs_t, gate_t, up_t, sig_t, hidden_t = forward(all_packed[t])
        _, out_grad_t, pre_grad_t = backward(route_t, all_cots[t], gate_t, up_t, sig_t)
        all_inputs.append(inputs_t)
        all_hidden.append(hidden_t)
        all_grads.append(out_grad_t)
        all_pre.append(pre_grad_t)

    pair = [(i, i ^ 1) for i in range(replicas)]

    def columns(values, side):
        size = values.shape[-1] // replicas
        return lax.dynamic_slice_in_dim(values, (place * CORES + side) * size, size, 2)

    def gradient(left, right):
        right = jnp.concatenate(right, axis=1)

        def part(side):
            chosen_columns = jnp.concatenate([columns(l, side) for l in left], axis=1)
            return jnp.einsum("era,erb->eab", chosen_columns, right, preferred_element_type=F32)

        share = with_layout_constraint(part(1 - core).astype(BF).swapaxes(0, 1), Layout((0, 1, 2)))
        theirs = lax.ppermute(share, "replica", pair)
        own = with_layout_constraint(part(core).swapaxes(0, 1), Layout((0, 1, 2)))
        return own + theirs.astype(F32)

    down_gradient = gradient(all_hidden, all_grads)
    gate_up_gradient = gradient(all_inputs, all_pre)

    slot_prob = jnp.sum(raw_cot.astype(F32) * outputs.astype(F32), axis=2).reshape(local, sources, cap, 1)
    prob_part = jnp.sum(jnp.where(chosen, slot_prob, 0.0), axis=2).swapaxes(0, 1)
    choice = expert_ids.T
    prob_gradient = jnp.zeros((top, count), F32)
    home = lax.axis_index("expert")
    for s in range(sources):
        block = lax.rem(home + s, sources) * local
        theirs = to_source(prob_part[s], -s)
        hit = choice[:, None, :] == (block + jnp.arange(local, dtype=jnp.int32))[None, :, None]
        prob_gradient = prob_gradient + jnp.sum(jnp.where(hit, theirs[None], 0.0), axis=1)
    prob_gradient = prob_gradient.T
    return (combined, token_gradient, prob_gradient, gate_up_gradient, down_gradient)


HALF = 8
SPLIT = 3
FWD, BWD, FAR, JOIN = 24, 24, 28, 8


def routing_tile(note_refs, expert, count, cap):
    members, weights = [], []
    for ref in note_refs:
        tile = ref[...].astype(F32)
        named = tile[:, :count].astype(jnp.int32) == expert
        members.append(jnp.max(jnp.where(named, 1.0, 0.0), axis=0, keepdims=True))
        weights.append(jnp.sum(jnp.where(named, tile[:, count:], 0.0), axis=0, keepdims=True))
    member = jnp.concatenate(members, axis=0)
    ahead = (
        lax.broadcasted_iota(jnp.int32, (count, count), 0) < lax.broadcasted_iota(jnp.int32, (count, count), 1)
    )
    ahead = jnp.where(ahead, 1.0, 0.0).astype(BF)
    rank = jnp.dot(member.astype(BF), ahead, preferred_element_type=F32).astype(jnp.int32)
    slots = len(note_refs) * cap
    row = lax.broadcasted_iota(jnp.int32, (slots, count), 0)
    picks = []
    for s in range(len(note_refs)):
        place = jnp.where(members[s] > 0.0, rank[s:s + 1] + s * cap, -1)
        picks.append(row == place)
    return picks, weights


def selected(picks, values):
    return jnp.concatenate([jnp.where(p, v, 0.0) for p, v in zip(picks, values)], axis=1)


def across(left, right):
    return lax.dot_general(left, right, (((0,), (0,)), ((), ())), preferred_element_type=F32)


def against(left, right):
    return lax.dot_general(left, right, (((1,), (1,)), ((), ())), preferred_element_type=F32)


def forward_tile(pick, tok, gate_ref, hidden_width):
    inputs = jnp.dot(pick, tok[...], preferred_element_type=F32).astype(BF)
    pre_act = jnp.dot(inputs, gate_ref[0], preferred_element_type=F32)
    gate, up = pre_act[:, :hidden_width], pre_act[:, hidden_width:]
    sig = jax.nn.sigmoid(gate)
    return inputs, pre_act, (gate * sig * up).astype(BF)


def backward_tile(pick, back, cot, down_ref, pre_act, hidden_width):
    raw_cot = jnp.dot(pick, cot[...], preferred_element_type=F32)
    out_grad = (jnp.sum(back, axis=1, keepdims=True) * raw_cot).astype(BF)
    hidden_grad = against(out_grad, down_ref[0])
    gate, up = pre_act[:, :hidden_width], pre_act[:, hidden_width:]
    sig = jax.nn.sigmoid(gate)
    pre_grad = jnp.concatenate(
        [hidden_grad * up * sig * (1.0 + gate * (1.0 - sig)), hidden_grad * gate * sig], axis=1
    ).astype(BF)
    return raw_cot, out_grad, pre_grad


def own_forward(sources, cap, info, *refs):
    packed, refs = refs[:sources], refs[sources:]
    note_refs, refs = refs[:sources], refs[sources:]
    gate_ref, down_ref, refs = refs[0], refs[1], refs[2:]
    part_refs, refs = refs[:sources], refs[sources:]
    input_ref, pre_ref, hidden_ref, output_ref, tok, total = refs
    e = pl.program_id(0)
    count = tok.shape[0] // sources

    @pl.when(e == 0)
    def _():
        for s in range(sources):
            tok[s * count:(s + 1) * count, :] = packed[s][...]
        total[...] = jnp.zeros_like(total)

    picks, weights = routing_tile(note_refs, info[0] + e, count, cap)
    pick = selected(picks, [1.0] * sources).astype(BF)
    back = selected(picks, weights)
    inputs, pre_act, hidden = forward_tile(pick, tok, gate_ref, hidden_ref.shape[2])
    outputs = jnp.dot(hidden, down_ref[0], preferred_element_type=F32).astype(BF)
    input_ref[0] = inputs
    pre_ref[0] = pre_act
    hidden_ref[0] = hidden
    output_ref[0] = outputs
    total[...] += across(back.astype(BF), outputs)

    @pl.when(e == pl.num_programs(0) - 1)
    def _():
        for s in range(sources):
            part_refs[s][...] = total[s * count:(s + 1) * count, :].astype(BF)


def own_backward(sources, cap, info, *refs):
    cots, refs = refs[:sources], refs[sources:]
    note_refs, refs = refs[:sources], refs[sources:]
    gate_ref, down_ref, pre_ref, output_ref, refs = refs[0], refs[1], refs[2], refs[3], refs[4:]
    part_refs, refs = refs[:sources], refs[sources:]
    out_grad_ref, pre_grad_ref, cot, total, prob = refs
    e = pl.program_id(0)
    count = cot.shape[0] // sources

    @pl.when(e == 0)
    def _():
        for s in range(sources):
            cot[s * count:(s + 1) * count, :] = cots[s][...]
        total[...] = jnp.zeros_like(total)
        prob[...] = jnp.zeros_like(prob)

    picks, weights = routing_tile(note_refs, info[0] + e, count, cap)
    pick = selected(picks, [1.0] * sources).astype(BF)
    back = selected(picks, weights)
    hidden_width = pre_ref.shape[2] // 2
    raw_cot, out_grad, pre_grad = backward_tile(pick, back, cot, down_ref, pre_ref[0], hidden_width)
    out_grad_ref[0] = out_grad
    pre_grad_ref[0] = pre_grad
    slot_prob = jnp.sum(raw_cot * output_ref[0].astype(F32), axis=1, keepdims=True)
    for s in range(sources):
        prob[s, pl.ds(e, 1), :] = jnp.sum(jnp.where(picks[s], slot_prob, 0.0), axis=0, keepdims=True)
    input_grad = against(pre_grad, gate_ref[0]).astype(BF)
    total[...] += across(pick, input_grad)

    @pl.when(e == pl.num_programs(0) - 1)
    def _():
        for s in range(sources):
            part_refs[s][:count, :] = total[s * count:(s + 1) * count, :].astype(BF)
            part_refs[s][count:, :] = jnp.zeros((HALF, total.shape[1]), BF)
            left = prob[s]
            for i in range(SPLIT):
                piece = left.astype(BF)
                part_refs[s][count:, i * count:(i + 1) * count] = piece
                left = left - piece.astype(F32)


def far_gradients(sources, cap, info, *refs):
    packed, refs = refs[:sources], refs[sources:]
    note_refs, refs = refs[:sources], refs[sources:]
    cots, refs = refs[:sources], refs[sources:]
    gate_ref, down_ref, input_ref, hidden_ref, out_grad_ref, pre_grad_ref = refs[:6]
    gate_own, gate_share, down_own, down_share = refs[6:10]
    tok, cot, all_inputs, all_hidden, all_grads, all_pre, down_sum = refs[10:]
    e = pl.program_id(0)
    count = tok.shape[0] // sources
    slots = sources * cap

    @pl.when(e == 0)
    def _():
        for s in range(sources):
            tok[s * count:(s + 1) * count, :] = packed[s][...]
            cot[s * count:(s + 1) * count, :] = cots[s][...]

    picks, weights = routing_tile(note_refs, info[0] + e, count, cap)
    pick = selected(picks, [1.0] * sources).astype(BF)
    back = selected(picks, weights)
    hidden_width = hidden_ref.shape[2]
    inputs, pre_act, hidden = forward_tile(pick, tok, gate_ref, hidden_width)
    _, out_grad, pre_grad = backward_tile(pick, back, cot, down_ref, pre_act, hidden_width)
    for scratch, own, far in (
        (all_inputs, input_ref, inputs), (all_hidden, hidden_ref, hidden),
        (all_grads, out_grad_ref, out_grad), (all_pre, pre_grad_ref, pre_grad),
    ):
        scratch[:slots, :] = own[0]
        scratch[slots:, :] = far

    place, core = info[1], info[2]

    def block(index, size):
        return pl.ds(pl.multiple_of(index * size, size), size)

    size = gate_own.shape[1]
    gate_own[0] = across(all_inputs[:, block(place * CORES + core, size)], all_pre[...])
    gate_share[0] = across(all_inputs[:, block(place * CORES + 1 - core, size)], all_pre[...]).astype(BF)
    size = down_own.shape[1]
    down_sum[...] = across(all_hidden[:, block(place, CORES * size)], all_grads[...])
    down_own[0] = down_sum[block(core, size), :]
    down_share[0] = down_sum[block(1 - core, size), :].astype(BF)


def joined(local, gate_own, gate_share, down_own, down_share, gate_out, down_out):
    for own, share, out in ((gate_own, gate_share, gate_out), (down_own, down_share, down_out)):
        for e in range(local):
            out[:, e, :] = own[e] + share[e].astype(F32)


def summed(sources, *refs):
    prob_out = refs[-1]
    for s in range(sources):
        tile = refs[2 * sources + s][...].astype(F32)
        count = prob_out.shape[2]
        prob_out[s] = sum(tile[:, i * count:(i + 1) * count] for i in range(SPLIT))
    for first, out in ((0, refs[-3]), (sources, refs[-2])):
        total = refs[first][...].astype(F32)
        for ref in refs[first + 1:first + sources]:
            total += ref[...].astype(F32)
        out[...] = total.astype(BF)


def whole(*shape):
    return pl.BlockSpec(shape, lambda e, info: (0,) * len(shape))


def each(*shape):
    return pl.BlockSpec((1,) + shape, lambda e, info: (e,) + (0,) * len(shape))


def kernel_call(body, grid, in_specs, out_specs, out_shape, scratch, flops, moved, grant):
    return pl.pallas_call(
        body,
        grid_spec=pltpu.PrefetchScalarGridSpec(
            num_scalar_prefetch=1, grid=(grid,), in_specs=in_specs, out_specs=out_specs, scratch_shapes=scratch
        ),
        out_shape=out_shape,
        compiler_params=pltpu.CompilerParams(vmem_limit_bytes=grant << 20),
        cost_estimate=pl.CostEstimate(flops=flops, bytes_accessed=moved, transcendentals=0),
    )


def two_chips(tokens, expert_ids, gate_probs, cotangent, gate_up, down_weights, *, sources, replicas):
    count, width = tokens.shape
    top = expert_ids.shape[1]
    local = gate_up.shape[1]
    hidden_width = down_weights.shape[0]
    pre_width = gate_up.shape[2]
    cap = min(CAP, count)
    along = replicas // CORES
    replica = lax.axis_index("replica")
    core, place = lax.rem(replica, CORES), lax.div(replica, CORES)
    home = lax.axis_index("expert")
    slots = sources * cap
    info = jnp.stack([home * local, place, core]).astype(jnp.int32)

    def to_mate(values, mask):
        return lax.ppermute(values, "expert", [(i, i ^ mask) for i in range(sources)]) if mask else values

    def to_chip(values):
        step = [
            (x * CORES + c, ((x + 1) % along) * CORES + c)
            for x in range(along) for c in range(CORES)
        ]
        return lax.ppermute(values, "replica", step)

    fill = ((0, HALF - top), (0, 0))
    notes = jnp.concatenate(
        [jnp.pad(expert_ids.T.astype(BF), fill, constant_values=-1), jnp.pad(gate_probs.T, fill)], axis=1
    )
    packed = jnp.concatenate([tokens, jnp.pad(notes, ((0, 0), (0, width - 2 * count)))], axis=0)

    far_own = to_chip(jnp.concatenate([packed, cotangent], axis=0))

    def gathered(values):
        held = [values] * sources
        for mask in range(1, sources):
            low = mask & -mask
            held[mask] = to_mate(held[mask - low], low)
        far = [to_chip(h) for h in held[1:]]
        return held, far

    near_packed, far_packed = gathered(packed)
    near_cots, far_cots = gathered(cotangent)
    far_packed = [far_own[:packed.shape[0]]] + far_packed
    far_cots = [far_own[packed.shape[0]:]] + far_cots

    always = lax.optimization_barrier(jnp.ones((), jnp.bool_))

    def in_hbm(values):
        return pltpu.with_memory_space_constraint(values, pltpu.HBM)

    def by_expert(weights):
        moved = with_layout_constraint(weights.swapaxes(0, 1), Layout((0, 1, 2)))
        return lax.optimization_barrier(moved)

    down_rows = by_expert(down_weights)
    gate_rows = by_expert(jnp.where(always, gate_up, jnp.zeros((), BF)))

    block_specs = [whole(count, width)] * sources
    note_specs = [pl.BlockSpec((HALF, 2 * count), lambda e, info: (count // HALF, 0))] * sources
    weight_specs = [each(width, pre_width), each(hidden_width, width)]
    block_shape = jax.ShapeDtypeStruct((count, width), BF)
    gathered_rows = pltpu.VMEM((sources * count, width), BF)
    part_total = pltpu.VMEM((sources * count, width), F32)

    def array(size, dtype, rows=slots):
        return jax.ShapeDtypeStruct((local, rows, size), dtype)

    product = 2 * local * slots * width * hidden_width
    weight_bytes = 6 * local * width * hidden_width
    *out_parts, inputs, pre_act, hidden, outputs = kernel_call(
        functools.partial(own_forward, sources, cap),
        local,
        block_specs + note_specs + weight_specs,
        block_specs + [each(slots, width), each(slots, pre_width), each(slots, hidden_width), each(slots, width)],
        [block_shape] * sources + [array(width, BF), array(pre_width, F32), array(hidden_width, BF), array(width, BF)],
        [gathered_rows, part_total],
        4 * product,
        2 * weight_bytes,
        FWD,
    )(info, *near_packed, *near_packed, in_hbm(gate_rows), in_hbm(down_rows))

    def returned(parts):
        return [to_mate(parts[s], s) for s in range(sources)]

    out_arrived = returned(out_parts)

    *grad_parts, out_grad, pre_grad = kernel_call(
        functools.partial(own_backward, sources, cap),
        local,
        block_specs + note_specs + weight_specs + [each(slots, pre_width), each(slots, width)],
        [whole(count + HALF, width)] * sources + [each(slots, width), each(slots, pre_width)],
        [jax.ShapeDtypeStruct((count + HALF, width), BF)] * sources + [array(width, BF), array(pre_width, BF)],
        [gathered_rows, part_total, pltpu.VMEM((sources, HALF, count), F32)],
        4 * product,
        2 * weight_bytes,
        BWD,
    )(info, *near_cots, *near_packed, gate_rows, down_rows, pre_act, outputs)
    grad_arrived = returned(grad_parts)

    gate_block, down_block = width // replicas, hidden_width // replicas
    gate_own, gate_share, down_own, down_share = kernel_call(
        functools.partial(far_gradients, sources, cap),
        local,
        block_specs + note_specs + block_specs + weight_specs + [
            each(slots, width), each(slots, hidden_width), each(slots, width), each(slots, pre_width)
        ],
        [
            each(gate_block, pre_width), each(gate_block, pre_width),
            each(down_block, width), each(down_block, width),
        ],
        [
            pltpu.HBM((local, gate_block, pre_width), F32), array(pre_width, BF, gate_block),
            array(width, F32, down_block), array(width, BF, down_block),
        ],
        [
            gathered_rows, gathered_rows,
            pltpu.VMEM((2 * slots, width), BF), pltpu.VMEM((2 * slots, hidden_width), BF),
            pltpu.VMEM((2 * slots, width), BF), pltpu.VMEM((2 * slots, pre_width), BF),
            pltpu.VMEM((CORES * down_block, width), F32),
        ],
        6 * product,
        3 * weight_bytes,
        FAR,
    )(
        info, *far_packed, *far_packed, *far_cots, in_hbm(gate_rows), in_hbm(down_rows),
        inputs, hidden, out_grad, pre_grad,
    )

    pair = [(i, i ^ 1) for i in range(replicas)]
    down_theirs, gate_theirs = lax.ppermute(down_share, "replica", pair), lax.ppermute(gate_share, "replica", pair)

    combined, token_gradient, prob_theirs = pl.pallas_call(
        functools.partial(summed, sources),
        name="summed",
        grid=(2,),
        in_specs=[pl.BlockSpec((count // 2, width), lambda i: (i, 0))] * (2 * sources)
        + [pl.BlockSpec((HALF, width), lambda i: (count // HALF, 0))] * sources,
        out_specs=[pl.BlockSpec((count // 2, width), lambda i: (i, 0))] * 2
        + [pl.BlockSpec((sources, HALF, count), lambda i: (0, 0, 0))],
        out_shape=[block_shape] * 2 + [jax.ShapeDtypeStruct((sources, HALF, count), F32)],
        compiler_params=pltpu.CompilerParams(vmem_limit_bytes=JOIN << 20),
        cost_estimate=pl.CostEstimate(flops=0, bytes_accessed=20 * count * width, transcendentals=0),
    )(*out_arrived, *grad_arrived, *grad_arrived)

    cuts = 8
    gate_cut, down_cut = gate_block // cuts, down_block // cuts

    def near_spec(cut, size):
        return pl.BlockSpec((local, cut, size), lambda i: (0, i, 0))

    def out_spec(cut, size):
        return pl.BlockSpec((cut, local, size), lambda i: (i, 0, 0))

    gate_up_gradient, down_gradient = pl.pallas_call(
        functools.partial(joined, local),
        name="joined",
        grid=(cuts,),
        in_specs=[near_spec(gate_cut, pre_width)] * 2 + [near_spec(down_cut, width)] * 2,
        out_specs=[out_spec(gate_cut, pre_width), out_spec(down_cut, width)],
        out_shape=[
            jax.ShapeDtypeStruct((gate_block, local, pre_width), F32),
            jax.ShapeDtypeStruct((down_block, local, width), F32),
        ],
        compiler_params=pltpu.CompilerParams(vmem_limit_bytes=JOIN << 20),
        cost_estimate=pl.CostEstimate(flops=0, bytes_accessed=10 * gate_own.size, transcendentals=0),
    )(in_hbm(gate_own), gate_theirs, down_own, down_theirs)

    choice = expert_ids.T
    prob_gradient = jnp.zeros((top, count), F32)
    for s in range(sources):
        block = jnp.bitwise_xor(home, s) * local
        hit = choice[:, None, :] == (block + jnp.arange(local, dtype=jnp.int32))[None, :, None]
        theirs = prob_theirs[s, :local]
        prob_gradient = prob_gradient + jnp.sum(jnp.where(hit, theirs[None], 0.0), axis=1)
    return (combined, token_gradient, prob_gradient.T, gate_up_gradient, down_gradient)


def on_device(*args, sources, replicas):
    count, top, local = args[0].shape[0], args[1].shape[1], args[4].shape[1]
    small = sources * min(CAP, count) * local <= 1024 and sources <= 4
    plain = replicas == 2 * CORES and small and sources & (sources - 1) == 0 and local <= HALF and SPLIT * count <= args[0].shape[1] and args[0].shape[1] % (128 * replicas) == 0 and count % 128 == 0 and top <= HALF and 2 * count <= args[0].shape[1]
    return (two_chips if plain else general)(*args, sources=sources, replicas=replicas)


def solution(mesh):
    rows = P(("groups", "expert", "replica"), None)
    sources, replicas = mesh.shape["expert"], mesh.shape["replica"]

    def body(*args):
        return on_device(*args, sources=sources, replicas=replicas)

    return jax.shard_map(
        body,
        mesh=mesh,
        in_specs=(rows, rows, rows, rows, P(None, "expert", None), P(None, "expert", None)),
        out_specs=(
            rows,
            rows,
            rows,
            P(("groups", "replica"), "expert", None),
            P(("groups", "replica"), "expert", None),
        ),
        check_vma=False,
    )
```
